256 devices in a mesh: dp: 8 (over y, x_lo), seq: 32 (over x_hi, z, core).
Axes of the slice: x: 4 (x_hi: 2, x_lo: 2; x = x_hi * 2 + x_lo), y: 4, z: 8, core: 2. Of those that a mesh axis runs over, the one named last changes fastest.
Arguments:
- query_rows: bfloat16 [8, 6144, 512], P('dp', 'seq'), may hold values from -6 to 6
- key_rows: bfloat16 [8, 6144, 512], P('dp', 'seq'), may hold values from -6 to 6
- value_rows: bfloat16 [8, 6144, 512], P('dp', 'seq'), may hold values from -6 to 6
- attention_out: bfloat16 [8, 6144, 512], P('dp', 'seq'), may hold values from -6 to 6
- softmax_log: bfloat16 [8, 6144, 8], P('dp', 'seq'), as said below
- valid_lengths: int32 [8], replicated, may hold values from 3072 to 6144, as said below
- mixer_input: bfloat16 [8, 6144, 1024], P('dp', 'seq'), may hold values from -6 to 6
- upstream_grad: bfloat16 [8, 6144, 1024], P('dp', 'seq'), may hold values from -6 to 6
- output_proj: bfloat16 [512, 1024], replicated, may hold values from -0.25 to 0.25
- depth_kernel: float32 [31, 1024], replicated, may hold values from -1 to 1
Outputs:
- grad_queries: bfloat16 [8, 6144, 512], P('dp', 'seq')
- grad_keys: bfloat16 [8, 6144, 512], P('dp', 'seq')
- grad_values: bfloat16 [8, 6144, 512], P('dp', 'seq')
- grad_state: bfloat16 [8, 6144, 1024], P('dp', 'seq')
- grad_proj: float32 [512, 1024], replicated
- grad_kernel: float32 [31, 1024], replicated
The draws below stay inside these ranges and needn't reach their ends.
Inputs may be any that keep to these rules, and one draw needn't show every extreme that they name: `valid_lengths`: at least one recording has all 6144 frames valid. `softmax_log`: values lie between the logarithm of 6144 and that plus 1.5.
All inputs are finite; a program needn't handle non-finite values.
Results may differ from the reference program's by a relative error of at most 0.03.
Values may be sent and summed in bfloat16 or wider, within the bound.
No kernel may reach another device: no remote copies, remote signals or barrier semaphores. Data moves between devices by JAX's collectives and lax.ppermute only.
A program may use at most 192 MiB of HBM per device.

```python
import jax
import jax.numpy as jnp
from jax import lax

D = 1024
HEADS = 8
KERNEL = 31
HD = 512
FRAMES = 6144
REC = 8


def draw_softmax_log(key, part):
    base_log = jnp.log(jnp.float32(FRAMES))
    extra = 0.2 + 0.8 * jax.random.uniform(key, (REC, FRAMES, HEADS), jnp.float32)
    return (base_log + extra).astype(jnp.bfloat16)


def draw_valid_lengths(key, part):
    drawn = jax.random.randint(key, (REC,), FRAMES // 2, FRAMES + 1)
    filled = jax.random.randint(jax.random.fold_in(key, 7), (), 0, REC)
    return jnp.where(jnp.arange(REC) == filled, FRAMES, drawn).astype(jnp.int32)


def levels(rng, extent, split, smallest, largest):
    def one(position, parts):
        heights = jax.random.uniform(jax.random.fold_in(jax.random.fold_in(rng, 6), position), (parts,), jnp.float32, smallest / len(split), largest / len(split))
        return jnp.repeat(jnp.exp(heights), extent[position] // parts).reshape((-1,) + (1,) * (len(extent) - position - 1))

    gain = one(*split[0])
    for cut in split[1:]:
        gain = gain * one(*cut)
    return gain


def normal_values(rng, dims, deviation, most, shards=(), kind=jnp.bfloat16):
    array = deviation * jax.random.normal(rng, dims, jnp.float32)
    if shards:
        array = array * levels(rng, dims, shards, -0.22, 0.18)
    return jnp.clip(array, -most, most).astype(kind)


def setup_inputs(seed: int = 0) -> dict:
    key_of = jax.random.split(jax.random.key(seed), 11)
    return {
        "query_rows": normal_values(key_of[0], (REC, FRAMES, HD), 1.0, 6.0, ((0, 8), (1, 32))),
        "key_rows": normal_values(key_of[1], (REC, FRAMES, HD), 1.0, 6.0, ((0, 8), (1, 32))),
        "value_rows": normal_values(key_of[2], (REC, FRAMES, HD), 1.0, 6.0, ((0, 8), (1, 32))),
        "attention_out": normal_values(key_of[3], (REC, FRAMES, HD), 1.0, 6.0, ((0, 8), (1, 32))),
        "softmax_log": draw_softmax_log(jax.random.fold_in(key_of[10], 71), 0),
        "valid_lengths": draw_valid_lengths(jax.random.fold_in(key_of[10], 71), 0),
        "mixer_input": normal_values(key_of[6], (REC, FRAMES, D), 1.0, 6.0, ((0, 8), (1, 32))),
        "upstream_grad": normal_values(key_of[7], (REC, FRAMES, D), 1.0, 6.0, ((0, 8), (1, 32))),
        "output_proj": normal_values(key_of[8], (HD, D), HD ** -0.5, 0.25),
        "depth_kernel": normal_values(key_of[9], (KERNEL, D), KERNEL ** -0.5, 1.0, (), jnp.float32),
    }


def taps_forward(padded, tap_weights, row_count):

    def add_tap(tap_index, running_sum):
        window = lax.dynamic_slice_in_dim(padded, tap_index, row_count, 0).astype(jnp.float32)
        return running_sum + tap_weights[tap_index] * window
    return lax.fori_loop(0, tap_weights.shape[0], add_tap, jnp.zeros((row_count, padded.shape[1]), jnp.float32))

def taps_backward(padded_grad, tap_weights, row_count):
    last_tap = tap_weights.shape[0] - 1

    def add_tap(tap_index, running_sum):
        window = lax.dynamic_slice_in_dim(padded_grad, last_tap - tap_index, row_count, 0).astype(jnp.float32)
        return running_sum + tap_weights[tap_index] * window
    return lax.fori_loop(0, tap_weights.shape[0], add_tap, jnp.zeros((row_count, padded_grad.shape[1]), jnp.float32))

def taps_product(padded, grad_rows, row_count, tap_count):
    grad_float = grad_rows.astype(jnp.float32)

    def one_tap(tap_index):
        window = lax.dynamic_slice_in_dim(padded, tap_index, row_count, 0).astype(jnp.float32)
        return lax.optimization_barrier(jnp.sum(window * grad_float, axis=0))
    return lax.map(one_tap, jnp.arange(tap_count, dtype=jnp.int32))

def swish_grad(conv_pre, masked_grad):
    sigmoid_pre = jax.nn.sigmoid(conv_pre)
    return (masked_grad.astype(jnp.float32) * sigmoid_pre * (1.0 + conv_pre * (1.0 - sigmoid_pre))).astype(jnp.bfloat16)

def halve(values):
    return lax.optimization_barrier(values.astype(jnp.bfloat16)).astype(jnp.float32)

def attention_backward(query_rows, key_rows, value_rows, grad_out, attention_out, softmax_log, key_mask):
    frames, proj_width = query_rows.shape
    head_count = softmax_log.shape[1]
    head_size = proj_width // head_count
    query_heads = query_rows.astype(jnp.float32).reshape(frames, head_count, head_size)
    key_heads = key_rows.astype(jnp.float32).reshape(frames, head_count, head_size)
    value_heads = value_rows.astype(jnp.float32).reshape(frames, head_count, head_size)
    grad_heads = grad_out.astype(jnp.float32).reshape(frames, head_count, head_size)
    out_heads = attention_out.astype(jnp.float32).reshape(frames, head_count, head_size)
    delta_rows = halve(lax.optimization_barrier(jnp.sum(grad_heads * out_heads, axis=-1)))
    log_rows = softmax_log.astype(jnp.float32)
    block_rows = min(512, frames)
    block_count = frames // block_rows

    def one_block(running, block_index):
        grad_keys, grad_values = running
        first_row = block_index * block_rows
        query_block = lax.dynamic_slice_in_dim(query_heads, first_row, block_rows, 0)
        grad_block = lax.dynamic_slice_in_dim(grad_heads, first_row, block_rows, 0)
        delta_block = lax.dynamic_slice_in_dim(delta_rows, first_row, block_rows, 0)
        log_block = lax.dynamic_slice_in_dim(log_rows, first_row, block_rows, 0)
        scores = jnp.einsum('thd,uhd->htu', query_block, key_heads) * 0.125
        soft_probs = jnp.exp(scores - log_block.T[:, :, None]) * key_mask[None, None, :]
        grad_probs = jnp.einsum('thd,uhd->htu', grad_block, value_heads)
        grad_scores = halve(soft_probs * (grad_probs - delta_block.T[:, :, None]))
        probs_half = halve(soft_probs)
        grad_query = jnp.einsum('htu,uhd->thd', grad_scores, key_heads) * 0.125
        grad_keys = grad_keys + jnp.einsum('htu,thd->uhd', grad_scores, query_block)
        grad_values = grad_values + jnp.einsum('htu,thd->uhd', probs_half, grad_block)
        return ((grad_keys, grad_values), grad_query)
    zeros_heads = jnp.zeros((frames, head_count, head_size), jnp.float32)
    sums, query_blocks = lax.scan(one_block, (zeros_heads, zeros_heads), jnp.arange(block_count, dtype=jnp.int32))
    grad_queries = query_blocks.reshape(frames, proj_width).astype(jnp.bfloat16)
    grad_keys = (sums[0] * 0.125).reshape(frames, proj_width).astype(jnp.bfloat16)
    grad_values = sums[1].reshape(frames, proj_width).astype(jnp.bfloat16)
    return (grad_queries, grad_keys, grad_values)

def reference(query_rows, key_rows, value_rows, attention_out, softmax_log, valid_lengths, mixer_input, upstream_grad, output_proj, depth_kernel):
    tap_count = depth_kernel.shape[0]
    rim_width = tap_count // 2
    frames = query_rows.shape[1]
    positions = jnp.arange(frames, dtype=jnp.int32)
    proj_sum = jnp.zeros(output_proj.shape, jnp.float32)
    kernel_sum = jnp.zeros(depth_kernel.shape, jnp.float32)
    query_list, key_list, value_list, state_list = ([], [], [], [])
    for record in range(query_rows.shape[0]):
        keep_mask = (positions < valid_lengths[record]).astype(jnp.float32)
        keep_half = keep_mask.astype(jnp.bfloat16)[:, None]
        masked_in = mixer_input[record] * keep_half
        masked_grad = upstream_grad[record] * keep_half
        padded = jnp.pad(masked_in, ((rim_width, rim_width), (0, 0)))
        conv_pre = taps_forward(padded, depth_kernel, frames)
        grad_pre = swish_grad(conv_pre, masked_grad)
        padded_grad = jnp.pad(grad_pre, ((rim_width, rim_width), (0, 0)))
        conv_back = taps_backward(padded_grad, depth_kernel, frames)
        kernel_sum = kernel_sum + taps_product(padded, grad_pre, frames, tap_count)
        grad_state = (masked_grad.astype(jnp.float32) + keep_mask[:, None] * conv_back).astype(jnp.bfloat16)
        grad_out = jnp.dot(grad_state, output_proj.T, preferred_element_type=jnp.float32).astype(jnp.bfloat16)
        proj_sum = proj_sum + jnp.dot(attention_out[record].T, grad_state, preferred_element_type=jnp.float32)
        grad_q, grad_k, grad_v = attention_backward(query_rows[record], key_rows[record], value_rows[record], grad_out, attention_out[record], softmax_log[record], keep_mask)
        query_list.append(grad_q)
        key_list.append(grad_k)
        value_list.append(grad_v)
        state_list.append(grad_state)
    grad_scale = 1.0 / jnp.sqrt(jnp.sum(valid_lengths).astype(jnp.float32))
    return (jnp.stack(query_list), jnp.stack(key_list), jnp.stack(value_list), jnp.stack(state_list), proj_sum * grad_scale, kernel_sum * grad_scale)
```

```python
import functools

import jax
import jax.numpy as jnp
from jax import lax
from jax.experimental import pallas as pl
from jax.experimental.pallas import tpu as pltpu
from jax.sharding import Mesh, PartitionSpec as P

BF = jnp.bfloat16
F32 = jnp.float32
NT = (((1,), (1,)), ((), ()))
NN = (((1,), (0,)), ((), ()))
TN = (((0,), (0,)), ((), ()))
ROWS = 192
HALF = 96
HEADS = 8
HSIZE = 64
TAPS = 31
ALL = ("dp", "xh", "z", "core")
SEQ = ("xh", "z", "core")
VMEM_LIMIT = 56 << 20


def call(kernel, out_shape, cost=None, **kw):
    return pl.pallas_call(
        kernel,
        out_shape=out_shape,
        compiler_params=pltpu.CompilerParams(vmem_limit_bytes=VMEM_LIMIT),
        cost_estimate=cost,
        **kw,
    )


def sds(shape, dtype=BF):
    return jax.ShapeDtypeStruct(shape, dtype)


def pack_early(q_ref, k_ref, v_ref, o_ref):
    for h in range(HEADS):
        cols = slice(h * HSIZE, (h + 1) * HSIZE)
        o_ref[h, 0:ROWS, 0:HSIZE] = k_ref[0, :, cols]
        o_ref[h, 0:ROWS, HSIZE:128] = v_ref[0, :, cols]
        q = q_ref[0, :, cols] * BF(0.125)
        o_ref[h, ROWS : ROWS + HALF, 0:HSIZE] = q[:HALF]
        o_ref[h, ROWS : ROWS + HALF, HSIZE:128] = q[HALF:]


def conv_kernel(
    pos_ref,
    x_ref,
    g_ref,
    lo_ref,
    hi_ref,
    w_ref,
    proj_ref,
    attn_ref,
    log_ref,
    gs_ref,
    pk_ref,
    late_ref,
    xs,
    gm,
    gp,
    out_acc,
    attn_t,
    tmp,
):
    step = pl.program_id(0)
    first_row = pos_ref[0]
    length = pos_ref[1]

    @pl.when(step == 0)
    def _():
        out_acc[...] = jnp.zeros_like(out_acc)
        attn_t[...] = attn_ref[0].T

    def mask(rows, offset):
        at = first_row + offset + lax.broadcasted_iota(jnp.int32, (rows, 128), 0)
        return jnp.where((at >= 0) & (at < length), 1.0, 0.0).astype(F32)

    mask_x = mask(256, -32)
    mask_g = mask(224, -16)
    for half in range(2):
        cols = slice(half * 128, half * 128 + 128)
        xs[0:32, :] = lo_ref[0:32, cols].astype(F32) * mask_x[0:32]
        xs[32:224, :] = x_ref[0, :, cols].astype(F32) * mask_x[32:224]
        xs[224:256, :] = hi_ref[0:32, cols].astype(F32) * mask_x[224:256]
        gm[0:16, :] = lo_ref[32:48, cols].astype(F32) * mask_g[0:16]
        gm[16:208, :] = g_ref[0, :, cols].astype(F32) * mask_g[16:208]
        gm[208:224, :] = hi_ref[32:48, cols].astype(F32) * mask_g[208:224]
        pre = jnp.zeros((224, 128), F32)
        for j in range(TAPS):
            pre = pre + w_ref[j : j + 1, cols] * xs[1 + j : 225 + j, :]
        s = jax.nn.sigmoid(pre)
        gp[...] = (gm[...] * s * (1.0 + pre * (1.0 - s))).astype(BF).astype(F32)
        back = jnp.zeros((ROWS, 128), F32)
        for j in range(TAPS):
            back = back + w_ref[j : j + 1, cols] * gp[31 - j : 223 - j, :]
        gs = (gm[16:208, :] + mask_g[16:208] * back).astype(BF)
        gs_ref[0, :, cols] = gs
        out_acc[...] += lax.dot_general(
            gs, proj_ref[:, cols], NT, preferred_element_type=F32
        )
        pk_ref[half, 0:512, :] = lax.dot_general(
            attn_t[...], gs, NN, preferred_element_type=F32
        ).astype(BF)
        own = gp[16:208, :]
        rows = [
            jnp.sum(xs[17 + j : 209 + j, :] * own, axis=0, keepdims=True) for j in range(TAPS)
        ]
        rows.append(jnp.zeros((1, 128), F32))
        pk_ref[half, 512:544, :] = jnp.concatenate(rows, axis=0).astype(BF)

    @pl.when(step == pl.num_programs(0) - 1)
    def _():
        grad = out_acc[...].astype(BF)
        tmp[0:ROWS, :] = grad.astype(F32) * attn_ref[0].astype(F32)
        tmp[ROWS:256, :] = jnp.zeros((256 - ROWS, 512), F32)
        turned = tmp[...].T
        tmp[0:ROWS, 0:128] = jnp.concatenate(
            [log_ref[0].astype(F32), jnp.zeros((ROWS, 120), F32)], axis=1
        )
        logs = tmp[:, 0:128].T
        for h in range(HEADS):
            delta = jnp.sum(turned[h * HSIZE : (h + 1) * HSIZE], axis=0, keepdims=True)
            log_row = logs[h : h + 1]
            part = grad[:, h * HSIZE : (h + 1) * HSIZE]
            late_ref[h, 0:HALF, 0:HSIZE] = part[:HALF]
            late_ref[h, 0:HALF, HSIZE:128] = part[HALF:]
            late_ref[h, HALF : HALF + 16, :] = jnp.concatenate(
                [
                    delta[:, 0:128],
                    delta[:, 128:256],
                    log_row[:, 0:128],
                    log_row[:, 128:256],
                    jnp.zeros((12, 128), F32),
                ],
                axis=0,
            ).astype(BF)


def conv_call(pos, x, g, lo, hi, w, proj, attn, log):
    chunk = lambda i, *_: (0, 0, i)
    flat = lambda i, *_: (0, i)
    full3 = lambda i, *_: (0, 0, 0)
    return pl.pallas_call(
        conv_kernel,
        out_shape=(
            sds((1, ROWS, 1024)),
            sds((8, 544, 128)),
            sds((HEADS, HALF + 16, 128)),
        ),
        grid_spec=pltpu.PrefetchScalarGridSpec(
            num_scalar_prefetch=1,
            grid=(4,),
            in_specs=[
                pl.BlockSpec((1, ROWS, 256), chunk),
                pl.BlockSpec((1, ROWS, 256), chunk),
                pl.BlockSpec((48, 256), flat),
                pl.BlockSpec((48, 256), flat),
                pl.BlockSpec((TAPS, 256), flat),
                pl.BlockSpec((512, 256), flat),
                pl.BlockSpec((1, ROWS, 512), full3),
                pl.BlockSpec((1, ROWS, HEADS), full3),
            ],
            out_specs=[
                pl.BlockSpec((1, ROWS, 256), chunk),
                pl.BlockSpec((2, 544, 128), lambda i, *_: (i, 0, 0)),
                pl.BlockSpec((HEADS, HALF + 16, 128), full3),
            ],
            scratch_shapes=[
                pltpu.VMEM((256, 128), F32),
                pltpu.VMEM((224, 128), F32),
                pltpu.VMEM((224, 128), F32),
                pltpu.VMEM((ROWS, 512), F32),
                pltpu.VMEM((512, ROWS), BF),
                pltpu.VMEM((256, 512), F32),
            ],
        ),
        compiler_params=pltpu.CompilerParams(vmem_limit_bytes=VMEM_LIMIT),
    )(pos, x, g, lo, hi, w, proj, attn, log)


CALLS = 8
CHUNK = HEADS * ROWS
KEYS = 2 * CHUNK // CALLS
BT = 1024


def unpack_rows(x, blk, dst):
    left, right = x[:, 0:HSIZE], x[:, HSIZE:128]
    dst[blk * 128 : blk * 128 + 96, :] = left
    dst[blk * 128 + 96 : blk * 128 + 128, :] = right[0:32]
    dst[2048 + blk * 64 : 2048 + blk * 64 + 64, :] = right[32:96]


def prep_early(pos_ref, own_ref, qc_ref, kvx_ref, q_ref, k_ref, v_ref, kt_ref, kf):
    length = pos_ref[0]
    for z in range(8):
        unpack_rows(own_ref[z, ROWS : ROWS + HALF, :], z, q_ref)
        unpack_rows(qc_ref[z], 8 + z, q_ref)
    for c in range(2):
        for z in range(8):
            kv = kvx_ref[z] if c == 0 else own_ref[z, 0:ROWS, :]
            at = c * CHUNK + z * ROWS
            k_ref[at : at + ROWS, :] = kv[:, 0:HSIZE]
            v_ref[at : at + ROWS, :] = kv[:, HSIZE:128]
            row = pos_ref[1 + c] + z * 2 * ROWS
            row = row + lax.broadcasted_iota(jnp.int32, (ROWS, 128), 0)
            kf[at : at + ROWS, :] = jnp.where(row < length, kv.astype(F32) * 0.125, 0.0)
    for b in range(2 * CHUNK // 512):
        turned = kf[b * 512 : b * 512 + 512, :].T
        kt_ref[:, b * 512 : b * 512 + 512] = turned[0:HSIZE].astype(BF)


def prep_late(own_ref, core_ref, do_ref, st_ref):
    stats = []
    for c, ref in enumerate((own_ref, core_ref)):
        for z in range(8):
            blk = c * 8 + z
            unpack_rows(ref[z, 0:HALF, :], blk, do_ref)
            st = ref[z, HALF : HALF + 16, :].astype(F32)
            st_ref[0:1, blk * 128 : blk * 128 + 128] = st[0:1]
            st_ref[1:2, blk * 128 : blk * 128 + 128] = st[2:3]
            stats.append(st)
    lane = lax.broadcasted_iota(jnp.int32, (1, 128), 1)
    for m in range(8):
        a, b = stats[2 * m], stats[2 * m + 1]
        at = 2048 + m * 128
        for row in range(2):
            src = 2 * row + 1
            st_ref[row : row + 1, at : at + 128] = jnp.where(
                lane < 64, a[src : src + 1], pltpu.roll(b[src : src + 1], 64, 1)
            )


def attn_kernel(first, part, pos_ref, q, do, st, k, v, kt, *rest):
    dqt = rest[-1]
    dkv_ref = rest[-2]
    if first:
        dqt[...] = jnp.zeros_like(dqt)
    else:
        dqt[...] = rest[0][...]
    kb, vb, ktb = k[...], v[...], kt[...]

    def query_block(ti, carry):
        dk, dv = carry
        t0 = pl.multiple_of(ti * BT, BT)
        qb = q[pl.ds(t0, BT), :]
        dob = do[pl.ds(t0, BT), :]
        s = lax.dot_general(kb, qb, NT, preferred_element_type=F32)
        p = jnp.exp(s - st[1:2, pl.ds(t0, BT)])
        dp = lax.dot_general(vb, dob, NT, preferred_element_type=F32)
        ds = (p * (dp - st[0:1, pl.ds(t0, BT)])).astype(BF)
        dv = dv + lax.dot_general(p.astype(BF), dob, NN, preferred_element_type=F32)
        dk = dk + lax.dot_general(ds, qb, NN, preferred_element_type=F32)
        dqt[:, pl.ds(t0, BT)] += lax.dot_general(ktb, ds, NN, preferred_element_type=F32)
        return dk, dv

    zero = jnp.zeros((KEYS, HSIZE), F32)
    dk, dv = lax.fori_loop(0, 2 * CHUNK // BT, query_block, (zero, zero))
    c, z0 = divmod(part * KEYS // ROWS, 8)
    for i in range(KEYS // ROWS):
        row = pos_ref[1 + c] + (z0 + i) * 2 * ROWS
        row = row + lax.broadcasted_iota(jnp.int32, (ROWS, HSIZE), 0)
        keep = row < pos_ref[0]
        rows = slice(i * ROWS, i * ROWS + ROWS)
        dkv_ref[i, :, 0:HSIZE] = jnp.where(keep, dk[rows], 0.0).astype(BF)
        dkv_ref[i, :, HSIZE:128] = jnp.where(keep, dv[rows], 0.0).astype(BF)


def attn_call(part, pos, q, do, st, k, v, kt, dqt):
    first = dqt is None
    full = lambda *_: (0, 0)
    rows = lambda *_: (part, 0)
    specs = [
        pl.BlockSpec((2 * CHUNK, HSIZE), full),
        pl.BlockSpec((2 * CHUNK, HSIZE), full),
        pl.BlockSpec((8, 2 * CHUNK), full),
        pl.BlockSpec((KEYS, HSIZE), rows),
        pl.BlockSpec((KEYS, HSIZE), rows),
        pl.BlockSpec((HSIZE, KEYS), lambda *_: (0, part)),
    ]
    args = [pos, q, do, st, k, v, kt]
    if not first:
        specs.append(pl.BlockSpec((HSIZE, 2 * CHUNK), full))
        args.append(dqt)
    scores = KEYS * 2 * CHUNK
    return pl.pallas_call(
        functools.partial(attn_kernel, first, part),
        out_shape=(sds((KEYS // ROWS, ROWS, 128)), sds((HSIZE, 2 * CHUNK), F32)),
        grid_spec=pltpu.PrefetchScalarGridSpec(
            num_scalar_prefetch=1,
            grid=(1,),
            in_specs=specs,
            out_specs=[
                pl.BlockSpec((KEYS // ROWS, ROWS, 128), lambda *_: (0, 0, 0)),
                pl.BlockSpec((HSIZE, 2 * CHUNK), full),
            ],
        ),
        input_output_aliases={} if first else {7: 1},
        compiler_params=pltpu.CompilerParams(vmem_limit_bytes=VMEM_LIMIT),
        cost_estimate=pl.CostEstimate(
            flops=10 * scores * 256, transcendentals=scores, bytes_accessed=4 << 20
        ),
    )(*args)


def turn_queries(dqt_ref, own_ref, core_ref, dq):
    for b in range(6):
        dq[b * 512 : b * 512 + 512, :] = dqt_ref[:, b * 512 : b * 512 + 512].T
    for c, ref in enumerate((own_ref, core_ref)):
        for z in range(8):
            blk = c * 8 + z
            ref[z, :, 0:HSIZE] = dq[blk * 128 : blk * 128 + 96, :].astype(BF)
            ref[z, 0:32, HSIZE:128] = dq[blk * 128 + 96 : blk * 128 + 128, :].astype(BF)
            ref[z, 32:96, HSIZE:128] = dq[2048 + blk * 64 : 2048 + blk * 64 + 64, :].astype(BF)


def unpack_final(x_ref, q_ref, k_ref, v_ref):
    for h in range(HEADS):
        cols = slice(h * HSIZE, (h + 1) * HSIZE)
        k_ref[0, :, cols] = x_ref[h, 0:ROWS, 0:HSIZE]
        v_ref[0, :, cols] = x_ref[h, 0:ROWS, HSIZE:128]
        q_ref[0, 0:HALF, cols] = x_ref[h, ROWS : ROWS + HALF, 0:HSIZE]
        q_ref[0, HALF:ROWS, cols] = x_ref[h, ROWS : ROWS + HALF, HSIZE:128]


def finish_sums(scale_ref, x_ref, proj_ref, taps_ref):
    scale = scale_ref[0]
    for c in range(8):
        cols = slice(c * 128, c * 128 + 128)
        proj_ref[:, cols] = x_ref[c, 0:512, :].astype(F32) * scale
        taps_ref[:, cols] = x_ref[c, 512:543, :].astype(F32) * scale


ROUNDS = (("core", 0), ("dp", 0), ("dp", 1), ("dp", 2), ("xh", 0), ("z", 0), ("z", 1), ("z", 2))


def partner(axis, bit):
    size = lax.axis_size(axis)
    return [(i, i ^ (1 << bit)) for i in range(size)]


def reduce_round(x, axis, bit):
    b = (lax.axis_index(axis) >> bit) & 1
    halves = x.reshape(2, x.shape[0] // 2, 128)
    send = lax.dynamic_index_in_dim(halves, 1 - b, 0, keepdims=False)
    keep = lax.dynamic_index_in_dim(halves, b, 0, keepdims=False)
    got = lax.ppermute(send, axis, partner(axis, bit))
    return (keep.astype(F32) + got.astype(F32)).astype(BF)


def gather_round(x, axis, bit):
    b = ((lax.axis_index(axis) >> bit) & 1) == 1
    got = lax.ppermute(x, axis, partner(axis, bit))
    return jnp.concatenate([jnp.where(b, got, x), jnp.where(b, x, got)], axis=0)


def swap(x, axis):
    return lax.ppermute(x, axis, [(0, 1), (1, 0)])


def shards(query, key, value, attn, log, lengths, x, g, proj, taps):
    xh, z, core = (lax.axis_index(a) for a in SEQ)
    index = (xh * 8 + z) * 2 + core
    length = lax.dynamic_index_in_dim(lengths, lax.axis_index("dp"), 0, keepdims=False)
    up = [(i, i + 1) for i in range(31)]
    down = [(i + 1, i) for i in range(31)]
    last = jnp.concatenate([x[0, 160:192], g[0, 176:192]], axis=0)
    first = jnp.concatenate([x[0, 0:32], g[0, 0:16]], axis=0)
    lo = lax.ppermute(last, SEQ, up)
    hi = lax.ppermute(first, SEQ, down)

    packed = call(pack_early, sds((HEADS, ROWS + HALF, 128)))(query, key, value)
    early = lax.all_to_all(packed, "z", 0, 0, tiled=True)
    qc = swap(early[:, ROWS:], "core")
    kvx = swap(early[:, :ROWS], "xh")
    own_row = (xh * 16 + core) * ROWS
    other_row = ((1 - xh) * 16 + core) * ROWS
    pos = jnp.stack([length, other_row, own_row]).astype(jnp.int32)
    smem = pl.BlockSpec(memory_space=pltpu.SMEM)
    vmem = pl.BlockSpec(memory_space=pltpu.VMEM)
    q, k, v, kt = call(
        prep_early,
        (sds((2 * CHUNK, HSIZE)),) * 3 + (sds((HSIZE, 2 * CHUNK)),),
        in_specs=[smem, vmem, vmem, vmem],
        scratch_shapes=[pltpu.VMEM((2 * CHUNK, 128), F32)],
    )(pos, early, qc, kvx)

    conv_pos = jnp.stack([index * ROWS, length]).astype(jnp.int32)
    grad_state, sums, late = conv_call(conv_pos, x, g, lo, hi, taps, proj, attn, log)
    late = lax.all_to_all(late, "z", 0, 0, tiled=True)
    late_core = swap(late, "core")
    do, st = call(prep_late, (sds((2 * CHUNK, HSIZE)), sds((8, 2 * CHUNK), F32)))(late, late_core)

    dqt = None
    dkv = []
    for part in range(CALLS):
        piece, dqt = attn_call(part, pos, q, do, st, k, v, kt, dqt)
        dkv.append(piece)
    dkv_other = swap(jnp.concatenate(dkv[: CALLS // 2], axis=0), "xh")
    dkv_own = jnp.concatenate(dkv[CALLS // 2 :], axis=0)
    dq_own, dq_core = call(
        turn_queries,
        (sds((8, HALF, 128)),) * 2,
        scratch_shapes=[pltpu.VMEM((2 * CHUNK, HSIZE), F32)],
    )(dqt)
    dq_core = swap(dq_core, "core")
    dkv_sum = (dkv_own.astype(F32) + dkv_other.astype(F32)).astype(BF)
    dq_sum = (dq_own.astype(F32) + dq_core.astype(F32)).astype(BF)
    back = lax.all_to_all(jnp.concatenate([dkv_sum, dq_sum], axis=1), "z", 0, 0, tiled=True)
    grad_q, grad_k, grad_v = call(unpack_final, (sds((1, ROWS, 512)),) * 3)(back)

    sums = sums.reshape(8 * 544, 128)
    for axis, bit in ROUNDS:
        sums = reduce_round(sums, axis, bit)
    for axis, bit in reversed(ROUNDS):
        sums = gather_round(sums, axis, bit)
    scale = 1.0 / jnp.sqrt(jnp.sum(lengths).astype(F32))
    grad_proj, grad_taps = call(
        finish_sums,
        (sds((512, 1024), F32), sds((TAPS, 1024), F32)),
        in_specs=[smem, vmem],
    )(scale.reshape(1), sums.reshape(8, 544, 128))
    return grad_q, grad_k, grad_v, grad_state, grad_proj, grad_taps


def solution(mesh):
    inner = Mesh(mesh.devices.reshape(8, 2, 8, 2), ALL)
    rows = P("dp", SEQ, None)
    in_specs = (rows,) * 5 + (P(), rows, rows, P(), P())
    out_specs = (rows,) * 4 + (P(), P())
    return jax.shard_map(
        shards, mesh=inner, in_specs=in_specs, out_specs=out_specs, check_vma=False
    )
```

```python
import functools

import jax
import jax.numpy as jnp
from jax import lax
from jax.experimental import pallas as pl
from jax.experimental.pallas import tpu as pltpu
from jax.sharding import Mesh, PartitionSpec as P

BF = jnp.bfloat16
F32 = jnp.float32
NT = (((1,), (1,)), ((), ()))
NN = (((1,), (0,)), ((), ()))
TN = (((0,), (0,)), ((), ()))
ROWS = 192
HALF = 96
HEADS = 8
HSIZE = 64
TAPS = 31
FREE = 60
WIDTH = 256
ALL = ("dp", "xh", "z", "core")
SEQ = ("xh", "z", "core")


def cost(micros):
    return pl.CostEstimate(flops=int(micros * 1.15e9), transcendentals=0, bytes_accessed=1 << 20)


def call(kernel, out_shape, micros, vmem, **kw):
    return pl.pallas_call(
        kernel,
        out_shape=out_shape,
        compiler_params=pltpu.CompilerParams(vmem_limit_bytes=vmem << 20),
        cost_estimate=cost(micros),
        **kw,
    )


def record_length(lengths_ref):
    return lengths_ref[lax.axis_index("dp")]


def sds(shape, dtype=BF):
    return jax.ShapeDtypeStruct(shape, dtype)


def pack_early(q_ref, k_ref, v_ref, xl_ref, xf_ref, gl_ref, gf_ref, o_ref, last_ref, first_ref):
    last_ref[0:32, :] = xl_ref[0]
    last_ref[32:48, :] = gl_ref[0]
    first_ref[0:32, :] = xf_ref[0]
    first_ref[32:48, :] = gf_ref[0]
    for h in range(HEADS):
        cols = slice(h * HSIZE, (h + 1) * HSIZE)
        o_ref[h, 0:ROWS, 0:HSIZE] = k_ref[0, :, cols]
        o_ref[h, 0:ROWS, HSIZE:128] = v_ref[0, :, cols]
        q = q_ref[0, :, cols] * BF(0.125)
        o_ref[h, ROWS : ROWS + HALF, 0:HSIZE] = q[:HALF]
        o_ref[h, ROWS : ROWS + HALF, HSIZE:128] = q[HALF:]


def pack_call(query, key, value, x, g):
    full = lambda i: (0, 0, 0)
    rows = pl.BlockSpec((1, ROWS, 512), full)
    rim = lambda n, at: pl.BlockSpec((1, n, 1024), lambda i: (0, at, 0))
    edge = pl.BlockSpec((48, 1024), lambda i: (0, 0))
    return call(
        pack_early,
        (sds((HEADS, ROWS + HALF, 128)), sds((48, 1024)), sds((48, 1024))),
        2,
        FREE,
        grid=(1,),
        in_specs=[rows, rows, rows, rim(32, 5), rim(32, 0), rim(16, 11), rim(16, 0)],
        out_specs=[pl.BlockSpec((HEADS, ROWS + HALF, 128), full), edge, edge],
    )(query, key, value, x, x, g, g)


def conv_kernel(
    lengths_ref,
    x_ref,
    g_ref,
    lo_ref,
    hi_ref,
    w_ref,
    proj_ref,
    attn_ref,
    log_ref,
    gs_ref,
    pk_ref,
    late_ref,
    xs,
    gm,
    gp,
    out_acc,
    attn_t,
    tmp,
):
    step = pl.program_id(0)
    first_row = lax.axis_index(SEQ) * ROWS
    length = record_length(lengths_ref)

    @pl.when(step == 0)
    def _():
        out_acc[...] = jnp.zeros_like(out_acc)
        attn_t[...] = attn_ref[0].T

    def mask(rows, offset):
        at = first_row + offset + lax.broadcasted_iota(jnp.int32, (rows, 128), 0)
        return jnp.where((at >= 0) & (at < length), 1.0, 0.0).astype(F32)

    mask_x = mask(256, -32)
    mask_g = mask(224, -16)
    for half in range(WIDTH // 128):
        cols = slice(half * 128, half * 128 + 128)
        xs[0:32, :] = lo_ref[0:32, cols].astype(F32) * mask_x[0:32]
        xs[32:224, :] = x_ref[0, :, cols].astype(F32) * mask_x[32:224]
        xs[224:256, :] = hi_ref[0:32, cols].astype(F32) * mask_x[224:256]
        gm[0:16, :] = lo_ref[32:48, cols].astype(F32) * mask_g[0:16]
        gm[16:208, :] = g_ref[0, :, cols].astype(F32) * mask_g[16:208]
        gm[208:224, :] = hi_ref[32:48, cols].astype(F32) * mask_g[208:224]
        pre = jnp.zeros((224, 128), F32)
        for j in range(TAPS):
            pre = pre + w_ref[j : j + 1, cols] * xs[1 + j : 225 + j, :]
        s = jax.nn.sigmoid(pre)
        gp[...] = (gm[...] * s * (1.0 + pre * (1.0 - s))).astype(BF).astype(F32)
        back = jnp.zeros((ROWS, 128), F32)
        for j in range(TAPS):
            back = back + w_ref[j : j + 1, cols] * gp[31 - j : 223 - j, :]
        gs = (gm[16:208, :] + mask_g[16:208] * back).astype(BF)
        gs_ref[0, :, cols] = gs
        out_acc[...] += lax.dot_general(
            gs, proj_ref[:, cols], NT, preferred_element_type=F32
        )
        pk_ref[half, 0:512, :] = lax.dot_general(
            attn_t[...], gs, NN, preferred_element_type=F32
        ).astype(BF)
        own = gp[16:208, :]
        rows = [
            jnp.sum(xs[17 + j : 209 + j, :] * own, axis=0, keepdims=True) for j in range(TAPS)
        ]
        rows.append(jnp.zeros((1, 128), F32))
        pk_ref[half, 512:544, :] = jnp.concatenate(rows, axis=0).astype(BF)

    @pl.when(step == pl.num_programs(0) - 1)
    def _():
        grad = out_acc[...].astype(BF)
        tmp[0:ROWS, :] = grad.astype(F32) * attn_ref[0].astype(F32)
        tmp[ROWS:256, :] = jnp.zeros((256 - ROWS, 512), F32)
        turned = tmp[...].T
        logs = jnp.concatenate(
            [log_ref[...].astype(F32), jnp.zeros((HEADS, 256 - ROWS), F32)], axis=1
        )
        for h in range(HEADS):
            delta = jnp.sum(turned[h * HSIZE : (h + 1) * HSIZE], axis=0, keepdims=True)
            log_row = logs[h : h + 1]
            part = grad[:, h * HSIZE : (h + 1) * HSIZE]
            late_ref[h, 0:HALF, 0:HSIZE] = part[:HALF]
            late_ref[h, 0:HALF, HSIZE:128] = part[HALF:]
            late_ref[h, HALF : HALF + 16, :] = jnp.concatenate(
                [
                    delta[:, 0:128],
                    delta[:, 128:256],
                    log_row[:, 0:128],
                    log_row[:, 128:256],
                    jnp.zeros((12, 128), F32),
                ],
                axis=0,
            ).astype(BF)


def conv_call(lengths, x, g, lo, hi, w, proj, attn, log):
    chunk = lambda i, *_: (0, 0, i)
    flat = lambda i, *_: (0, i)
    full3 = lambda i, *_: (0, 0, 0)
    full2 = lambda i, *_: (0, 0)
    return pl.pallas_call(
        conv_kernel,
        out_shape=(
            sds((1, ROWS, 1024)),
            sds((8, 544, 128)),
            sds((HEADS, HALF + 16, 128)),
        ),
        grid_spec=pltpu.PrefetchScalarGridSpec(
            num_scalar_prefetch=1,
            grid=(1024 // WIDTH,),
            in_specs=[
                pl.BlockSpec((1, ROWS, WIDTH), chunk),
                pl.BlockSpec((1, ROWS, WIDTH), chunk),
                pl.BlockSpec((48, WIDTH), flat),
                pl.BlockSpec((48, WIDTH), flat),
                pl.BlockSpec((TAPS, WIDTH), flat),
                pl.BlockSpec((512, WIDTH), flat),
                pl.BlockSpec((1, ROWS, 512), full3),
                pl.BlockSpec((HEADS, ROWS), full2),
            ],
            out_specs=[
                pl.BlockSpec((1, ROWS, WIDTH), chunk),
                pl.BlockSpec((WIDTH // 128, 544, 128), lambda i, *_: (i, 0, 0)),
                pl.BlockSpec((HEADS, HALF + 16, 128), full3),
            ],
            scratch_shapes=[
                pltpu.VMEM((256, 128), F32),
                pltpu.VMEM((224, 128), F32),
                pltpu.VMEM((224, 128), F32),
                pltpu.VMEM((ROWS, 512), F32),
                pltpu.VMEM((512, ROWS), BF),
                pltpu.VMEM((256, 512), F32),
            ],
        ),
        compiler_params=pltpu.CompilerParams(vmem_limit_bytes=FREE << 20),
        cost_estimate=cost(11),
    )(lengths, x, g, lo, hi, w, proj, attn, log)


CHUNK = HEADS * ROWS
BU = 512
BT = 1536


def key_rows(part, z, lanes):
    xh = lax.axis_index("xh")
    half = 1 - xh if part == 0 else xh
    row = ((half * 8 + z) * 2 + lax.axis_index("core")) * ROWS
    return row + lax.broadcasted_iota(jnp.int32, (ROWS, lanes), 0)


def unpack_rows(x, c, z, dst):
    left, right = x[:, 0:HSIZE], x[:, HSIZE:128]
    at = c * CHUNK + z * 128
    end = c * CHUNK + 1024 + z * 64
    dst[at : at + 96, :] = left
    dst[at + 96 : at + 128, :] = right[0:32]
    dst[end : end + 64, :] = right[32:96]


def turn_rows(dqt, dq, put):
    for b in range(3):
        dq[b * 512 : b * 512 + 512, :] = dqt[:, b * 512 : b * 512 + 512].T
    for z in range(8):
        at, end = z * 128, 1024 + z * 64
        put(z, slice(0, 96), slice(0, HSIZE), dq[at : at + 96, :])
        put(z, slice(0, 32), slice(HSIZE, 128), dq[at + 96 : at + 128, :])
        put(z, slice(32, 96), slice(HSIZE, 128), dq[end : end + 64, :])


def prep_early(lengths_ref, own_ref, qc_ref, kvx_ref, q_ref, k_ref, v_ref, kt_ref, kf):
    length = record_length(lengths_ref)
    for z in range(8):
        unpack_rows(own_ref[z, ROWS : ROWS + HALF, :], 0, z, q_ref)
        unpack_rows(qc_ref[z], 1, z, q_ref)
    for c in range(2):
        for z in range(8):
            kv = kvx_ref[z] if c == 0 else own_ref[z, 0:ROWS, :]
            at = c * CHUNK + z * ROWS
            k_ref[at : at + ROWS, :] = kv[:, 0:HSIZE]
            v_ref[at : at + ROWS, :] = kv[:, HSIZE:128]
            row = key_rows(c, z, 128)
            kf[at : at + ROWS, :] = jnp.where(row < length, kv.astype(F32) * 0.125, 0.0)
    for b in range(2 * CHUNK // 512):
        turned = kf[b * 512 : b * 512 + 512, :].T
        kt_ref[:, b * 512 : b * 512 + 512] = turned[0:HSIZE].astype(BF)


def prep_late(own_ref, core_ref, do_ref, st_ref):
    lane = lax.broadcasted_iota(jnp.int32, (1, 128), 1)
    for c, ref in enumerate((own_ref, core_ref)):
        stats = []
        for z in range(8):
            unpack_rows(ref[z, 0:HALF, :], c, z, do_ref)
            st = ref[z, HALF : HALF + 16, :].astype(F32)
            at = c * CHUNK + z * 128
            st_ref[0:1, at : at + 128] = st[0:1]
            st_ref[1:2, at : at + 128] = st[2:3]
            stats.append(st)
        for m in range(4):
            a, b = stats[2 * m], stats[2 * m + 1]
            at = c * CHUNK + 1024 + m * 128
            for row in range(2):
                src = 2 * row + 1
                st_ref[row : row + 1, at : at + 128] = jnp.where(
                    lane < 64, a[src : src + 1], pltpu.roll(b[src : src + 1], 64, 1)
                )


def score_tile(c, q, do, st, k, v, kt, dqt, dks, dvs):
    def key_block(ui, _):
        u0 = pl.multiple_of(ui * BU, BU)
        kb = k[pl.ds(u0, BU), :]
        vb = v[pl.ds(u0, BU), :]
        ktb = kt[:, pl.ds(u0, BU)]
        dk, dv = dks[pl.ds(u0, BU), :], dvs[pl.ds(u0, BU), :]
        for ti in range(CHUNK // BT):
            cols = slice(ti * BT, ti * BT + BT)
            at = slice(c * CHUNK + ti * BT, c * CHUNK + ti * BT + BT)
            qb = q[at, :]
            dob = do[at, :]
            s = lax.dot_general(kb, qb, NT, preferred_element_type=F32)
            p = jnp.exp(s - st[1:2, at])
            dp = lax.dot_general(vb, dob, NT, preferred_element_type=F32)
            ds = (p * (dp - st[0:1, at])).astype(BF)
            dv = dv + lax.dot_general(p.astype(BF), dob, NN, preferred_element_type=F32)
            dk = dk + lax.dot_general(ds, qb, NN, preferred_element_type=F32)
            dqt[:, cols] += lax.dot_general(ktb, ds, NN, preferred_element_type=F32)
        dks[pl.ds(u0, BU), :] = dk
        dvs[pl.ds(u0, BU), :] = dv
        return 0

    lax.fori_loop(0, CHUNK // BU, key_block, 0)


def tile_other_own(q, do, st, k, v, kt, dqo, dks, dvs):
    for ref in (dqo, dks, dvs):
        ref[...] = jnp.zeros_like(ref)
    score_tile(0, q, do, st, k, v, kt, dqo, dks, dvs)


def tile_other_core(lengths_ref, q, do, st, k, v, kt, dk_ref, dv_ref, dkv_ref, dqc, dks, dvs):
    dqc[...] = jnp.zeros_like(dqc)
    dks[...] = dk_ref[...]
    dvs[...] = dv_ref[...]
    score_tile(1, q, do, st, k, v, kt, dqc, dks, dvs)
    length = record_length(lengths_ref)
    for z in range(8):
        keep = key_rows(0, z, HSIZE) < length
        rows = slice(z * ROWS, z * ROWS + ROWS)
        dkv_ref[z, :, 0:HSIZE] = jnp.where(keep, dks[rows, :], 0.0).astype(BF)
        dkv_ref[z, :, HSIZE:128] = jnp.where(keep, dvs[rows, :], 0.0).astype(BF)


def tile_own_core(q, do, st, k, v, kt, dqc_ref, dq_ref, dks, dvs, dqt, dq):
    dks[...] = jnp.zeros_like(dks)
    dvs[...] = jnp.zeros_like(dvs)
    dqt[...] = dqc_ref[...]
    score_tile(1, q, do, st, k, v, kt, dqt, dks, dvs)

    def put(z, rows, cols, value):
        dq_ref[z, rows, cols] = value.astype(BF)

    turn_rows(dqt, dq, put)


def tile_own_own(q, do, st, k, v, kt, dqo_ref, dk_ref, dv_ref, dqt, dks, dvs):
    dqt[...] = dqo_ref[...]
    dks[...] = dk_ref[...]
    dvs[...] = dv_ref[...]
    score_tile(0, q, do, st, k, v, kt, dqt, dks, dvs)


def tile_call(body, part, lengths, tensors, extra, outs, scratch=()):
    full = lambda *_: (0, 0)
    whole = lambda x: pl.BlockSpec(x.shape, lambda *_: (0,) * len(x.shape))
    specs = [
        pl.BlockSpec((2 * CHUNK, HSIZE), full),
        pl.BlockSpec((2 * CHUNK, HSIZE), full),
        pl.BlockSpec((8, 2 * CHUNK), full),
        pl.BlockSpec((CHUNK, HSIZE), lambda *_: (part, 0)),
        pl.BlockSpec((CHUNK, HSIZE), lambda *_: (part, 0)),
        pl.BlockSpec((HSIZE, CHUNK), lambda *_: (0, part)),
    ] + [whole(e) for e in extra]
    args = list(tensors) + list(extra)
    if lengths is not None:
        specs.insert(0, pl.BlockSpec(memory_space=pltpu.SMEM))
        args.insert(0, lengths)
    return call(
        body,
        outs,
        7,
        40,
        grid=(1,),
        in_specs=specs,
        out_specs=tuple(whole(o) for o in outs),
        scratch_shapes=scratch,
    )(*args)


def combine(lengths_ref, dk_ref, dv_ref, got_ref, dqt_ref, dqgot_ref, o_ref, dq):
    length = record_length(lengths_ref)
    for z in range(8):
        keep = key_rows(1, z, HSIZE) < length
        rows = slice(z * ROWS, z * ROWS + ROWS)
        got = got_ref[z].astype(F32)
        dk = jnp.where(keep, dk_ref[rows, :], 0.0) + got[:, 0:HSIZE]
        dv = jnp.where(keep, dv_ref[rows, :], 0.0) + got[:, HSIZE:128]
        o_ref[z, 0:ROWS, 0:HSIZE] = dk.astype(BF)
        o_ref[z, 0:ROWS, HSIZE:128] = dv.astype(BF)

    def put(z, rows, cols, value):
        to = slice(ROWS + rows.start, ROWS + rows.stop)
        o_ref[z, to, cols] = (value + dqgot_ref[z, rows, cols].astype(F32)).astype(BF)

    turn_rows(dqt_ref, dq, put)


def unpack_final(x_ref, q_ref, k_ref, v_ref):
    for h in range(HEADS):
        cols = slice(h * HSIZE, (h + 1) * HSIZE)
        k_ref[0, :, cols] = x_ref[h, 0:ROWS, 0:HSIZE]
        v_ref[0, :, cols] = x_ref[h, 0:ROWS, HSIZE:128]
        q_ref[0, 0:HALF, cols] = x_ref[h, ROWS : ROWS + HALF, 0:HSIZE]
        q_ref[0, HALF:ROWS, cols] = x_ref[h, ROWS : ROWS + HALF, HSIZE:128]


def split_sums(x_ref, keep_ref, send_ref):
    core = lax.axis_index("core")
    keep_ref[...] = x_ref[pl.ds(core * 4, 4)]
    send_ref[...] = x_ref[pl.ds((1 - core) * 4, 4)]


def finish_sums(lengths_ref, own_ref, got_ref, proj_ref, taps_ref):
    total = lengths_ref[0]
    for r in range(1, 8):
        total = total + lengths_ref[r]
    scale = lax.rsqrt(jnp.full((1, 128), total, jnp.int32).astype(F32))
    core = lax.axis_index("core")
    for c in range(8):
        cols = slice(c * 128, c * 128 + 128)
        own, got = own_ref[c % 4].astype(F32), got_ref[c % 4].astype(F32)
        x = jnp.where(core == c // 4, own, got) * scale
        proj_ref[:, cols] = x[0:512]
        taps_ref[:, cols] = x[512:543]


def flip(x, axis, mask, size):
    return lax.ppermute(x, axis, [(i, i ^ mask) for i in range(size)])


def add(*terms):
    pair = [a.astype(F32) + b.astype(F32) for a, b in zip(terms[::2], terms[1::2])]
    return (pair[0] if len(pair) == 1 else pair[0] + pair[1]).astype(BF)


def reduce_dp(x, shift, count):
    me = (lax.axis_index("dp") >> shift) & (count - 1)
    pieces = x.reshape(count, x.shape[0] // count, 128)
    piece = lambda i: lax.dynamic_index_in_dim(pieces, i, 0, keepdims=False)
    got = [flip(piece(me ^ d), "dp", d << shift, 8) for d in range(1, count)]
    return add(piece(me), *got)


def sum_four(x, low, high):
    axes = ("xh", "z")
    return add(x, *[flip(x, axes, mask, 16) for mask in (low, high, low | high)])


def gather_y(x):
    y = lax.axis_index("dp") >> 1
    odd, upper = (y & 1) == 1, (y & 2) == 2
    a, b, c, d = (x, *[flip(x, "dp", m << 1, 8) for m in (1, 2, 3)])
    low = jnp.concatenate([jnp.where(odd, b, a), jnp.where(odd, a, b)], axis=0)
    high = jnp.concatenate([jnp.where(odd, d, c), jnp.where(odd, c, d)], axis=0)
    return jnp.concatenate([jnp.where(upper, high, low), jnp.where(upper, low, high)], axis=0)


def gather_x(x):
    odd = (lax.axis_index("dp") & 1) == 1
    got = flip(x, "dp", 1, 8)
    return jnp.concatenate([jnp.where(odd, got, x), jnp.where(odd, x, got)], axis=0)


def after(x, *first):
    return lax.optimization_barrier((x,) + first)[0]


def swap(x, axis):
    return lax.ppermute(x, axis, [(0, 1), (1, 0)])


def shards(query, key, value, attn, log, lengths, x, g, proj, taps):
    smem = pl.BlockSpec(memory_space=pltpu.SMEM)
    vmem = pl.BlockSpec(memory_space=pltpu.VMEM)
    up = [(i, i + 1) for i in range(31)]
    down = [(i + 1, i) for i in range(31)]
    packed, last, first = pack_call(query, key, value, x, g)
    lo = lax.ppermute(last, SEQ, up)
    hi = lax.ppermute(first, SEQ, down)
    early = lax.all_to_all(packed, "z", 0, 0, tiled=True)

    grad_state, sums, late = conv_call(lengths, x, g, lo, hi, taps, proj, attn, log[0].T)
    late = lax.all_to_all(after(late, early), "z", 0, 0, tiled=True)

    kvx = swap(early[:, :ROWS], "xh")
    qc = swap(early[:, ROWS:], "core")
    q, k, v, kt = call(
        prep_early,
        (sds((2 * CHUNK, HSIZE)),) * 3 + (sds((HSIZE, 2 * CHUNK)),),
        2,
        16,
        in_specs=[smem, vmem, vmem, vmem],
        scratch_shapes=[pltpu.VMEM((2 * CHUNK, 128), F32)],
    )(lengths, early, qc, kvx)

    keep, send = call(
        split_sums, (sds((4, 544, 128)),) * 2, 40, 8, in_specs=[vmem], out_specs=[vmem, vmem]
    )(after(sums, early))
    sums = add(keep, swap(send, "core")).reshape(2176, 128)
    sums = reduce_dp(after(sums, kvx), 0, 2)

    late_core = swap(late, "core")
    do, st = call(prep_late, (sds((2 * CHUNK, HSIZE)), sds((8, 2 * CHUNK), F32)), 1, 8)(
        late, late_core
    )
    do = after(do, sums)
    tensors = (q, do, st, k, v, kt)
    grad = sds((CHUNK, HSIZE), F32)
    turned = sds((HSIZE, CHUNK), F32)
    fgrad = pltpu.VMEM((CHUNK, HSIZE), F32)
    fturned = pltpu.VMEM((HSIZE, CHUNK), F32)
    sums = reduce_dp(sums, 1, 4)
    dqo, dk, dv = tile_call(tile_other_own, 0, None, tensors, (), (turned, grad, grad))
    dk = after(dk, sums)
    sums = sum_four(sums, 1, 8)
    dkv_other, dqc = tile_call(
        tile_other_core,
        0,
        lengths,
        tensors,
        (dk, dv),
        (sds((HEADS, ROWS, 128)), turned),
        [fgrad, fgrad],
    )
    dkv_got = swap(dkv_other, "xh")
    dqc = after(dqc, sums)
    sums = sum_four(sums, 2, 4)
    dq_core, dk, dv = tile_call(
        tile_own_core, 1, None, tensors, (dqc,), (sds((8, HALF, 128)), grad, grad), [fturned, fgrad]
    )
    dq_got = swap(dq_core, "core")
    dk = after(dk, sums, dkv_got)
    sums = gather_y(sums)
    dqo, dk, dv = tile_call(tile_own_own, 1, None, tensors, (dqo, dk, dv), (turned, grad, grad))
    dk = after(dk, sums)
    back = call(
        combine,
        sds((HEADS, ROWS + HALF, 128)),
        2,
        16,
        in_specs=[smem] + [vmem] * 5,
        scratch_shapes=[fgrad],
    )(lengths, dk, dv, dkv_got, dqo, dq_got)

    sums, back = lax.optimization_barrier((sums, back))
    back = lax.all_to_all(back, "z", 0, 0, tiled=True)
    sums = gather_x(sums).reshape(4, 544, 128)
    grad_proj, grad_taps = call(
        finish_sums,
        (sds((512, 1024), F32), sds((TAPS, 1024), F32)),
        2,
        8,
        in_specs=[smem, vmem, vmem],
    )(lengths, sums, swap(sums, "core"))
    grad_q, grad_k, grad_v = call(unpack_final, (sds((1, ROWS, 512)),) * 3, 2, 8)(back)
    return grad_q, grad_k, grad_v, grad_state, grad_proj, grad_taps


def solution(mesh):
    inner = Mesh(mesh.devices.reshape(8, 2, 8, 2), ALL)
    rows = P("dp", SEQ, None)
    in_specs = (rows,) * 5 + (P(), rows, rows, P(), P())
    out_specs = (rows,) * 4 + (P(), P())
    return jax.shard_map(
        shards, mesh=inner, in_specs=in_specs, out_specs=out_specs, check_vma=False
    )
```

```python
import functools

import jax
import jax.numpy as jnp
from jax import lax
from jax.experimental import pallas as pl
from jax.experimental.pallas import tpu as pltpu
from jax.sharding import Mesh, PartitionSpec as P

BF = jnp.bfloat16
F32 = jnp.float32
NT = (((1,), (1,)), ((), ()))
NN = (((1,), (0,)), ((), ()))
TN = (((0,), (0,)), ((), ()))
ROWS = 192
HALF = 96
HEADS = 8
HSIZE = 64
TAPS = 31
FREE = 60
WIDTH = 256
ALL = ("dp", "xh", "z", "core")
SEQ = ("xh", "z", "core")


def cost(micros):
    return pl.CostEstimate(flops=int(micros * 1.15e9), transcendentals=0, bytes_accessed=1 << 20)


def call(kernel, out_shape, micros, vmem, **kw):
    return pl.pallas_call(
        kernel,
        out_shape=out_shape,
        compiler_params=pltpu.CompilerParams(vmem_limit_bytes=vmem << 20),
        cost_estimate=cost(micros),
        **kw,
    )


def record_length(lengths_ref):
    return lengths_ref[lax.axis_index("dp")]


def sds(shape, dtype=BF):
    return jax.ShapeDtypeStruct(shape, dtype)


def rims(xl_ref, xf_ref, gl_ref, gf_ref, last_ref, first_ref):
    last_ref[0:32, :] = xl_ref[0]
    last_ref[32:48, :] = gl_ref[0]
    first_ref[0:32, :] = xf_ref[0]
    first_ref[32:48, :] = gf_ref[0]


def rims_call(x, g):
    rim = lambda n, at: pl.BlockSpec((1, n, 1024), lambda i: (0, at, 0))
    edge = pl.BlockSpec((48, 1024), lambda i: (0, 0))
    return call(
        rims,
        (sds((48, 1024)), sds((48, 1024))),
        1,
        FREE,
        grid=(1,),
        in_specs=[rim(32, 5), rim(32, 0), rim(16, 11), rim(16, 0)],
        out_specs=[edge, edge],
    )(x, x, g, g)


def conv_kernel(
    lengths_ref,
    x_ref,
    g_ref,
    lo_ref,
    hi_ref,
    w_ref,
    proj_ref,
    attn_ref,
    log_ref,
    q_ref,
    k_ref,
    v_ref,
    gs_ref,
    pk_ref,
    pay_ref,
    xs,
    gm,
    gp,
    out_acc,
    attn_t,
    tmp,
):
    step = pl.program_id(0)
    first_row = lax.axis_index(SEQ) * ROWS
    length = record_length(lengths_ref)

    @pl.when(step == 0)
    def _():
        out_acc[...] = jnp.zeros_like(out_acc)
        attn_t[...] = attn_ref[0].T

    for i in range(2):
        cols = slice(i * HSIZE, (i + 1) * HSIZE)
        h = pl.ds(2 * step + i, 1)
        pay_ref[h, 0:ROWS, 0:HSIZE] = k_ref[:, :, cols]
        pay_ref[h, 0:ROWS, HSIZE:128] = v_ref[:, :, cols]
        q = q_ref[:, :, cols] * BF(0.125)
        pay_ref[h, ROWS : ROWS + HALF, 0:HSIZE] = q[:, :HALF]
        pay_ref[h, ROWS : ROWS + HALF, HSIZE:128] = q[:, HALF:]

    def mask(rows, offset):
        at = first_row + offset + lax.broadcasted_iota(jnp.int32, (rows, 128), 0)
        return jnp.where((at >= 0) & (at < length), 1.0, 0.0).astype(F32)

    mask_x = mask(256, -32)
    mask_g = mask(224, -16)
    for half in range(WIDTH // 128):
        cols = slice(half * 128, half * 128 + 128)
        xs[0:32, :] = lo_ref[0:32, cols].astype(F32) * mask_x[0:32]
        xs[32:224, :] = x_ref[0, :, cols].astype(F32) * mask_x[32:224]
        xs[224:256, :] = hi_ref[0:32, cols].astype(F32) * mask_x[224:256]
        gm[0:16, :] = lo_ref[32:48, cols].astype(F32) * mask_g[0:16]
        gm[16:208, :] = g_ref[0, :, cols].astype(F32) * mask_g[16:208]
        gm[208:224, :] = hi_ref[32:48, cols].astype(F32) * mask_g[208:224]
        pre = jnp.zeros((224, 128), F32)
        for j in range(TAPS):
            pre = pre + w_ref[j : j + 1, cols] * xs[1 + j : 225 + j, :]
        s = jax.nn.sigmoid(pre)
        gp[...] = (gm[...] * s * (1.0 + pre * (1.0 - s))).astype(BF).astype(F32)
        back = jnp.zeros((ROWS, 128), F32)
        for j in range(TAPS):
            back = back + w_ref[j : j + 1, cols] * gp[31 - j : 223 - j, :]
        gs = (gm[16:208, :] + mask_g[16:208] * back).astype(BF)
        gs_ref[0, :, cols] = gs
        out_acc[...] += lax.dot_general(
            gs, proj_ref[:, cols], NT, preferred_element_type=F32
        )
        pk_ref[half, 0:512, :] = lax.dot_general(
            attn_t[...], gs, NN, preferred_element_type=F32
        ).astype(BF)
        own = gp[16:208, :]
        rows = [
            jnp.sum(xs[17 + j : 209 + j, :] * own, axis=0, keepdims=True) for j in range(TAPS)
        ]
        rows.append(jnp.zeros((1, 128), F32))
        pk_ref[half, 512:544, :] = jnp.concatenate(rows, axis=0).astype(BF)

    @pl.when(step == pl.num_programs(0) - 1)
    def _():
        grad = out_acc[...].astype(BF)
        tmp[0:ROWS, :] = grad.astype(F32) * attn_ref[0].astype(F32)
        tmp[ROWS:256, :] = jnp.zeros((256 - ROWS, 512), F32)
        turned = tmp[...].T
        logs = jnp.concatenate(
            [log_ref[...].astype(F32), jnp.zeros((HEADS, 256 - ROWS), F32)], axis=1
        )
        for h in range(HEADS):
            delta = jnp.sum(turned[h * HSIZE : (h + 1) * HSIZE], axis=0, keepdims=True)
            log_row = logs[h : h + 1]
            part = grad[:, h * HSIZE : (h + 1) * HSIZE]
            pay_ref[h, 288:384, 0:HSIZE] = part[:HALF]
            pay_ref[h, 288:384, HSIZE:128] = part[HALF:]
            pay_ref[h, 384:400, :] = jnp.concatenate(
                [
                    delta[:, 0:128],
                    delta[:, 128:256],
                    log_row[:, 0:128],
                    log_row[:, 128:256],
                    jnp.zeros((12, 128), F32),
                ],
                axis=0,
            ).astype(BF)


def conv_call(lengths, x, g, lo, hi, w, proj, attn, log, q, k, v):
    chunk = lambda i, *_: (0, 0, i)
    flat = lambda i, *_: (0, i)
    full3 = lambda i, *_: (0, 0, 0)
    full2 = lambda i, *_: (0, 0)
    return pl.pallas_call(
        conv_kernel,
        out_shape=(
            sds((1, ROWS, 1024)),
            sds((8, 544, 128)),
            sds((HEADS, 400, 128)),
        ),
        grid_spec=pltpu.PrefetchScalarGridSpec(
            num_scalar_prefetch=1,
            grid=(1024 // WIDTH,),
            in_specs=[
                pl.BlockSpec((1, ROWS, WIDTH), chunk),
                pl.BlockSpec((1, ROWS, WIDTH), chunk),
                pl.BlockSpec((48, WIDTH), flat),
                pl.BlockSpec((48, WIDTH), flat),
                pl.BlockSpec((TAPS, WIDTH), flat),
                pl.BlockSpec((512, WIDTH), flat),
                pl.BlockSpec((1, ROWS, 512), full3),
                pl.BlockSpec((HEADS, ROWS), full2),
                pl.BlockSpec((1, ROWS, 128), chunk),
                pl.BlockSpec((1, ROWS, 128), chunk),
                pl.BlockSpec((1, ROWS, 128), chunk),
            ],
            out_specs=[
                pl.BlockSpec((1, ROWS, WIDTH), chunk),
                pl.BlockSpec((WIDTH // 128, 544, 128), lambda i, *_: (i, 0, 0)),
                pl.BlockSpec((HEADS, 400, 128), full3),
            ],
            scratch_shapes=[
                pltpu.VMEM((256, 128), F32),
                pltpu.VMEM((224, 128), F32),
                pltpu.VMEM((224, 128), F32),
                pltpu.VMEM((ROWS, 512), F32),
                pltpu.VMEM((512, ROWS), BF),
                pltpu.VMEM((256, 512), F32),
            ],
        ),
        compiler_params=pltpu.CompilerParams(vmem_limit_bytes=FREE << 20),
        cost_estimate=cost(11),
    )(lengths, x, g, lo, hi, w, proj, attn, log, q, k, v)


CHUNK = HEADS * ROWS
BU = 512


def key_rows(part, z, lanes):
    xh = lax.axis_index("xh")
    half = 1 - xh if part == 0 else xh
    row = ((half * 8 + z) * 2 + lax.axis_index("core")) * ROWS
    return row + lax.broadcasted_iota(jnp.int32, (ROWS, lanes), 0)


def unpack_rows(x, z, dst):
    left, right = x[:, 0:HSIZE], x[:, HSIZE:128]
    at, end = z * 128, 1024 + z * 64
    dst[at : at + 96, :] = left
    dst[at + 96 : at + 128, :] = right[0:32]
    dst[end : end + 64, :] = right[32:96]


def turn_rows(dqt, dq, put):
    for b in range(3):
        dq[b * 512 : b * 512 + 512, :] = dqt[:, b * 512 : b * 512 + 512].T
    for z in range(8):
        at, end = z * 128, 1024 + z * 64
        put(z, slice(0, 96), slice(0, HSIZE), dq[at : at + 96, :])
        put(z, slice(0, 32), slice(HSIZE, 128), dq[at + 96 : at + 128, :])
        put(z, slice(32, 96), slice(HSIZE, 128), dq[end : end + 64, :])


def prep_queries(x_ref, q_ref, do_ref, st_ref):
    lane = lax.broadcasted_iota(jnp.int32, (1, 128), 1)
    stats = []
    for z in range(8):
        unpack_rows(x_ref[z, 0:HALF, :], z, q_ref)
        unpack_rows(x_ref[z, HALF:ROWS, :], z, do_ref)
        st = x_ref[z, ROWS : ROWS + 16, :].astype(F32)
        st_ref[0:1, z * 128 : z * 128 + 128] = st[0:1]
        st_ref[1:2, z * 128 : z * 128 + 128] = st[2:3]
        stats.append(st)
    for m in range(4):
        a, b = stats[2 * m], stats[2 * m + 1]
        at = 1024 + m * 128
        for row in range(2):
            src = 2 * row + 1
            st_ref[row : row + 1, at : at + 128] = jnp.where(
                lane < 64, a[src : src + 1], pltpu.roll(b[src : src + 1], 64, 1)
            )


def prep_keys(part, lengths_ref, x_ref, k_ref, v_ref, kt_ref, kf):
    length = record_length(lengths_ref)
    for z in range(8):
        kv = x_ref[z]
        rows = slice(z * ROWS, z * ROWS + ROWS)
        k_ref[rows, :] = kv[:, 0:HSIZE]
        v_ref[rows, :] = kv[:, HSIZE:128]
        kf[rows, :] = jnp.where(key_rows(part, z, 128) < length, kv.astype(F32) * 0.125, 0.0)
    for b in range(3):
        turned = kf[b * 512 : b * 512 + 512, :].T
        kt_ref[:, b * 512 : b * 512 + 512] = turned[0:HSIZE].astype(BF)


def score_tile(q, do, st, k, v, kt, dqt, dks, dvs):
    def key_block(ui, _):
        u0 = pl.multiple_of(ui * BU, BU)
        kb = k[pl.ds(u0, BU), :]
        vb = v[pl.ds(u0, BU), :]
        ktb = kt[:, pl.ds(u0, BU)]
        qb, dob = q[...], do[...]
        s = lax.dot_general(kb, qb, NT, preferred_element_type=F32)
        p = jnp.exp(s - st[1:2, :])
        dp = lax.dot_general(vb, dob, NT, preferred_element_type=F32)
        ds = (p * (dp - st[0:1, :])).astype(BF)
        dvs[pl.ds(u0, BU), :] += lax.dot_general(p.astype(BF), dob, NN, preferred_element_type=F32)
        dks[pl.ds(u0, BU), :] += lax.dot_general(ds, qb, NN, preferred_element_type=F32)
        dqt[...] += lax.dot_general(ktb, ds, NN, preferred_element_type=F32)
        return 0

    lax.fori_loop(0, CHUNK // BU, key_block, 0)


def tile_1(q, do, st, k, v, kt, dqt, dks, dvs):
    for ref in (dqt, dks, dvs):
        ref[...] = jnp.zeros_like(ref)
    score_tile(q, do, st, k, v, kt, dqt, dks, dvs)


def tile_2(q, do, st, k, v, kt, dq_ref, dqt, dks, dvs):
    dqt[...] = dq_ref[...]
    dks[...] = jnp.zeros_like(dks)
    dvs[...] = jnp.zeros_like(dvs)
    score_tile(q, do, st, k, v, kt, dqt, dks, dvs)


def tile_3(lengths_ref, q, do, st, k, v, kt, dk_ref, dv_ref, dkv_ref, dqt, dks, dvs):
    dqt[...] = jnp.zeros_like(dqt)
    dks[...] = dk_ref[...]
    dvs[...] = dv_ref[...]
    score_tile(q, do, st, k, v, kt, dqt, dks, dvs)
    length = record_length(lengths_ref)
    for z in range(8):
        keep = key_rows(0, z, HSIZE) < length
        rows = slice(z * ROWS, z * ROWS + ROWS)
        dkv_ref[z, :, 0:HSIZE] = jnp.where(keep, dks[rows, :], 0.0).astype(BF)
        dkv_ref[z, :, HSIZE:128] = jnp.where(keep, dvs[rows, :], 0.0).astype(BF)


def tile_4(q, do, st, k, v, kt, dq_in, dk_ref, dv_ref, dq_ref, dks, dvs, dqt, dq):
    dqt[...] = dq_in[...]
    dks[...] = dk_ref[...]
    dvs[...] = dv_ref[...]
    score_tile(q, do, st, k, v, kt, dqt, dks, dvs)

    def put(z, rows, cols, value):
        dq_ref[z, rows, cols] = value.astype(BF)

    turn_rows(dqt, dq, put)


def tile_call(body, lengths, args, outs, scratch=()):
    whole = lambda x: pl.BlockSpec(x.shape, lambda *_: (0,) * len(x.shape))
    specs = [whole(a) for a in args]
    if lengths is not None:
        specs.insert(0, pl.BlockSpec(memory_space=pltpu.SMEM))
        args = (lengths,) + args
    return call(
        body,
        outs,
        7,
        40,
        grid=(1,),
        in_specs=specs,
        out_specs=tuple(whole(o) for o in outs),
        scratch_shapes=scratch,
    )(*args)


def combine(lengths_ref, dk_ref, dv_ref, got_ref, dqt_ref, dqgot_ref, o_ref, dq):
    length = record_length(lengths_ref)
    for z in range(8):
        keep = key_rows(1, z, HSIZE) < length
        rows = slice(z * ROWS, z * ROWS + ROWS)
        got = got_ref[z].astype(F32)
        dk = jnp.where(keep, dk_ref[rows, :], 0.0) + got[:, 0:HSIZE]
        dv = jnp.where(keep, dv_ref[rows, :], 0.0) + got[:, HSIZE:128]
        o_ref[z, 0:ROWS, 0:HSIZE] = dk.astype(BF)
        o_ref[z, 0:ROWS, HSIZE:128] = dv.astype(BF)

    def put(z, rows, cols, value):
        to = slice(ROWS + rows.start, ROWS + rows.stop)
        o_ref[z, to, cols] = (value + dqgot_ref[z, rows, cols].astype(F32)).astype(BF)

    turn_rows(dqt_ref, dq, put)


def unpack_final(x_ref, q_ref, k_ref, v_ref):
    for h in range(HEADS):
        cols = slice(h * HSIZE, (h + 1) * HSIZE)
        k_ref[0, :, cols] = x_ref[h, 0:ROWS, 0:HSIZE]
        v_ref[0, :, cols] = x_ref[h, 0:ROWS, HSIZE:128]
        q_ref[0, 0:HALF, cols] = x_ref[h, ROWS : ROWS + HALF, 0:HSIZE]
        q_ref[0, HALF:ROWS, cols] = x_ref[h, ROWS : ROWS + HALF, HSIZE:128]


def finish_sums(lengths_ref, own_ref, got_ref, proj_ref, taps_ref):
    total = lengths_ref[0]
    for r in range(1, 8):
        total = total + lengths_ref[r]
    scale = lax.rsqrt(jnp.full((1, 128), total, jnp.int32).astype(F32))
    core = lax.axis_index("core")
    for c in range(8):
        cols = slice(c * 128, c * 128 + 128)
        own, got = own_ref[c % 4].astype(F32), got_ref[c % 4].astype(F32)
        x = jnp.where(core == c // 4, own, got) * scale
        proj_ref[:, cols] = x[0:512]
        taps_ref[:, cols] = x[512:543]


def flip(x, axis, mask, size):
    return lax.ppermute(x, axis, [(i, i ^ mask) for i in range(size)])


def add(*terms):
    pair = [a.astype(F32) + b.astype(F32) for a, b in zip(terms[::2], terms[1::2])]
    return (pair[0] if len(pair) == 1 else pair[0] + pair[1]).astype(BF)


def reduce_dp(x, shift, count):
    me = (lax.axis_index("dp") >> shift) & (count - 1)
    pieces = x.reshape(count, x.shape[0] // count, 128)
    piece = lambda i: lax.dynamic_index_in_dim(pieces, i, 0, keepdims=False)
    got = [flip(piece(me ^ d), "dp", d << shift, 8) for d in range(1, count)]
    return add(piece(me), *got)


def sum_four(x, low, high, beside):
    got = [flip(x, ("xh", "z"), mask, 16) for mask in (low, high, low | high)]
    return add(after(x, beside), *got)


def gather_y(x, beside):
    y = lax.axis_index("dp") >> 1
    odd, upper = (y & 1) == 1, (y & 2) == 2
    b, c, d = [flip(x, "dp", m << 1, 8) for m in (1, 2, 3)]
    a = after(x, beside)
    low = jnp.concatenate([jnp.where(odd, b, a), jnp.where(odd, a, b)], axis=0)
    high = jnp.concatenate([jnp.where(odd, d, c), jnp.where(odd, c, d)], axis=0)
    return jnp.concatenate([jnp.where(upper, high, low), jnp.where(upper, low, high)], axis=0)


def gather_x(x, beside):
    odd = (lax.axis_index("dp") & 1) == 1
    got = flip(x, "dp", 1, 8)
    x = after(x, beside)
    return jnp.concatenate([jnp.where(odd, got, x), jnp.where(odd, x, got)], axis=0)


def after(x, *first):
    return lax.optimization_barrier((x,) + first)[0]


def swap(x, axis):
    return lax.ppermute(x, axis, [(0, 1), (1, 0)])


def shards(query, key, value, attn, log, lengths, x, g, proj, taps):
    smem = pl.BlockSpec(memory_space=pltpu.SMEM)
    vmem = pl.BlockSpec(memory_space=pltpu.VMEM)
    up = [(i, i + 1) for i in range(31)]
    down = [(i + 1, i) for i in range(31)]
    last, first = rims_call(x, g)
    lo = lax.ppermute(last, SEQ, up)
    hi = lax.ppermute(first, SEQ, down)
    grad_state, sums, pay = conv_call(
        lengths, x, g, lo, hi, taps, proj, attn, log[0].T, query, key, value
    )
    pay = lax.all_to_all(pay, "z", 0, 0, tiled=True)

    core = lax.axis_index("core")
    sums = sums.reshape(2, 2176, 128)
    send = lax.dynamic_index_in_dim(sums, 1 - core, 0, keepdims=False)
    keep = lax.dynamic_index_in_dim(sums, core, 0, keepdims=False)
    sums = add(keep, swap(send, "core"))
    sums = reduce_dp(sums, 0, 2)
    sums = reduce_dp(sums, 1, 4)

    queries, keys = pay[:, ROWS:], pay[:, :ROWS]
    core_queries, other_keys = swap(queries, "core"), swap(keys, "xh")

    half = sds((CHUNK, HSIZE))

    def prepared_queries(x):
        return call(prep_queries, (half, half, sds((8, CHUNK), F32)), 1, 8)(x)

    def prepared_keys(part, x):
        return call(
            functools.partial(prep_keys, part),
            (half, half, sds((HSIZE, CHUNK))),
            1,
            8,
            in_specs=[smem, vmem],
            scratch_shapes=[pltpu.VMEM((CHUNK, 128), F32)],
        )(lengths, x)

    qo = prepared_queries(queries)
    ko = prepared_keys(1, keys)
    grad = sds((CHUNK, HSIZE), F32)
    turned = sds((HSIZE, CHUNK), F32)
    fgrad = pltpu.VMEM((CHUNK, HSIZE), F32)
    fturned = pltpu.VMEM((HSIZE, CHUNK), F32)
    dqo, dk, dv = tile_call(tile_1, None, qo + ko, (turned, grad, grad))
    sums = sum_four(sums, 1, 8, dk)

    kx = prepared_keys(0, other_keys)
    dqo = after(dqo, sums)
    dqo, dkx, dvx = tile_call(tile_2, None, qo + kx + (dqo,), (turned, grad, grad))
    sums = sum_four(sums, 2, 4, dvx)

    qc = prepared_queries(core_queries)
    dkx = after(dkx, sums)
    dkv_other, dqc = tile_call(
        tile_3, lengths, qc + kx + (dkx, dvx), (sds((HEADS, ROWS, 128)), turned), [fgrad, fgrad]
    )
    dkv_got = swap(dkv_other, "xh")
    sums = gather_y(sums, dqc)
    dqc = after(dqc, sums)
    dq_core, dk, dv = tile_call(
        tile_4,
        None,
        qc + ko + (dqc, dk, dv),
        (sds((8, HALF, 128)), grad, grad),
        [fturned, fgrad],
    )
    dq_got = swap(dq_core, "core")
    sums = gather_x(sums, dk)
    back = call(
        combine,
        sds((HEADS, ROWS + HALF, 128)),
        2,
        16,
        in_specs=[smem] + [vmem] * 5,
        scratch_shapes=[fgrad],
    )(lengths, dk, dv, dkv_got, dqo, dq_got)

    back = lax.all_to_all(back, "z", 0, 0, tiled=True)
    sums = sums.reshape(4, 544, 128)
    grad_proj, grad_taps = call(
        finish_sums,
        (sds((512, 1024), F32), sds((TAPS, 1024), F32)),
        2,
        8,
        in_specs=[smem, vmem, vmem],
    )(lengths, sums, swap(sums, "core"))
    grad_q, grad_k, grad_v = call(unpack_final, (sds((1, ROWS, 512)),) * 3, 2, 8)(back)
    return grad_q, grad_k, grad_v, grad_state, grad_proj, grad_taps


def solution(mesh):
    inner = Mesh(mesh.devices.reshape(8, 2, 8, 2), ALL)
    rows = P("dp", SEQ, None)
    in_specs = (rows,) * 5 + (P(), rows, rows, P(), P())
    out_specs = (rows,) * 4 + (P(), P())
    return jax.shard_map(
        shards, mesh=inner, in_specs=in_specs, out_specs=out_specs, check_vma=False
    )
```

```python
import functools

import jax
import jax.numpy as jnp
from jax import lax
from jax.experimental import pallas as pl
from jax.experimental.pallas import tpu as pltpu
from jax.sharding import Mesh, PartitionSpec as P

BF = jnp.bfloat16
F32 = jnp.float32
NT = (((1,), (1,)), ((), ()))
NN = (((1,), (0,)), ((), ()))
TN = (((0,), (0,)), ((), ()))
ROWS = 192
HALF = 96
HEADS = 8
HSIZE = 64
TAPS = 31
FREE = 60
WIDTH = 512
ALL = ("dp", "xh", "z", "core")
SEQ = ("xh", "z", "core")


def cost(micros):
    return pl.CostEstimate(flops=int(micros * 1.15e9), transcendentals=0, bytes_accessed=1 << 20)


def call(kernel, out_shape, micros, vmem, **kw):
    return pl.pallas_call(
        kernel,
        out_shape=out_shape,
        compiler_params=pltpu.CompilerParams(vmem_limit_bytes=vmem << 20),
        cost_estimate=cost(micros),
        **kw,
    )


def record_length(lengths_ref):
    return lengths_ref[lax.axis_index("dp")]


def sds(shape, dtype=BF):
    return jax.ShapeDtypeStruct(shape, dtype)


def rims(xl_ref, xf_ref, gl_ref, gf_ref, last_ref, first_ref):
    last_ref[0:32, :] = xl_ref[0]
    last_ref[32:48, :] = gl_ref[0]
    first_ref[0:32, :] = xf_ref[0]
    first_ref[32:48, :] = gf_ref[0]


def rims_call(x, g):
    rim = lambda n, at: pl.BlockSpec((1, n, 1024), lambda i: (0, at, 0))
    edge = pl.BlockSpec((48, 1024), lambda i: (0, 0))
    return call(
        rims,
        (sds((48, 1024)), sds((48, 1024))),
        1,
        FREE,
        grid=(1,),
        in_specs=[rim(32, 5), rim(32, 0), rim(16, 11), rim(16, 0)],
        out_specs=[edge, edge],
    )(x, x, g, g)


def conv_kernel(
    lengths_ref,
    x_ref,
    g_ref,
    lo_ref,
    hi_ref,
    w_ref,
    proj_ref,
    attn_ref,
    log_ref,
    q_ref,
    k_ref,
    v_ref,
    gs_ref,
    pk_ref,
    pay_ref,
    xs,
    gm,
    gp,
    out_acc,
    attn_t,
    tmp,
):
    step = pl.program_id(0)
    first_row = lax.axis_index(SEQ) * ROWS
    length = record_length(lengths_ref)

    @pl.when(step == 0)
    def _():
        out_acc[...] = jnp.zeros_like(out_acc)
        attn_t[...] = attn_ref[0].T

    heads = WIDTH // 128
    for i in range(heads):
        cols = slice(i * HSIZE, (i + 1) * HSIZE)
        h = pl.ds(heads * step + i, 1)
        pay_ref[h, 0:ROWS, 0:HSIZE] = k_ref[:, :, cols]
        pay_ref[h, 0:ROWS, HSIZE:128] = v_ref[:, :, cols]
        q = q_ref[:, :, cols] * BF(0.125)
        pay_ref[h, ROWS : ROWS + HALF, 0:HSIZE] = q[:, :HALF]
        pay_ref[h, ROWS : ROWS + HALF, HSIZE:128] = q[:, HALF:]

    def mask(rows, offset):
        at = first_row + offset + lax.broadcasted_iota(jnp.int32, (rows, 128), 0)
        return jnp.where((at >= 0) & (at < length), 1.0, 0.0).astype(F32)

    mask_x = mask(256, -32)
    mask_g = mask(224, -16)
    for half in range(WIDTH // 128):
        cols = slice(half * 128, half * 128 + 128)
        xs[0:32, :] = lo_ref[0:32, cols].astype(F32) * mask_x[0:32]
        xs[32:224, :] = x_ref[0, :, cols].astype(F32) * mask_x[32:224]
        xs[224:256, :] = hi_ref[0:32, cols].astype(F32) * mask_x[224:256]
        gm[0:16, :] = lo_ref[32:48, cols].astype(F32) * mask_g[0:16]
        gm[16:208, :] = g_ref[0, :, cols].astype(F32) * mask_g[16:208]
        gm[208:224, :] = hi_ref[32:48, cols].astype(F32) * mask_g[208:224]
        pre = jnp.zeros((224, 128), F32)
        for j in range(TAPS):
            pre = pre + w_ref[j : j + 1, cols] * xs[1 + j : 225 + j, :]
        s = jax.nn.sigmoid(pre)
        gp[...] = (gm[...] * s * (1.0 + pre * (1.0 - s))).astype(BF).astype(F32)
        back = jnp.zeros((ROWS, 128), F32)
        for j in range(TAPS):
            back = back + w_ref[j : j + 1, cols] * gp[31 - j : 223 - j, :]
        gs = (gm[16:208, :] + mask_g[16:208] * back).astype(BF)
        gs_ref[0, :, cols] = gs
        out_acc[...] += lax.dot_general(
            gs, proj_ref[:, cols], NT, preferred_element_type=F32
        )
        pk_ref[half, 0:512, :] = lax.dot_general(
            attn_t[...], gs, NN, preferred_element_type=F32
        ).astype(BF)
        own = gp[16:208, :]
        rows = [
            jnp.sum(xs[17 + j : 209 + j, :] * own, axis=0, keepdims=True) for j in range(TAPS)
        ]
        rows.append(jnp.zeros((1, 128), F32))
        pk_ref[half, 512:544, :] = jnp.concatenate(rows, axis=0).astype(BF)

    @pl.when(step == pl.num_programs(0) - 1)
    def _():
        grad = out_acc[...].astype(BF)
        tmp[0:ROWS, :] = grad.astype(F32) * attn_ref[0].astype(F32)
        tmp[ROWS:256, :] = jnp.zeros((256 - ROWS, 512), F32)
        turned = tmp[...].T
        logs = jnp.concatenate(
            [log_ref[...].astype(F32), jnp.zeros((HEADS, 256 - ROWS), F32)], axis=1
        )
        for h in range(HEADS):
            delta = jnp.sum(turned[h * HSIZE : (h + 1) * HSIZE], axis=0, keepdims=True)
            log_row = logs[h : h + 1]
            part = grad[:, h * HSIZE : (h + 1) * HSIZE]
            pay_ref[h, 288:384, 0:HSIZE] = part[:HALF]
            pay_ref[h, 288:384, HSIZE:128] = part[HALF:]
            pay_ref[h, 384:400, :] = jnp.concatenate(
                [
                    delta[:, 0:128],
                    delta[:, 128:256],
                    log_row[:, 0:128],
                    log_row[:, 128:256],
                    jnp.zeros((12, 128), F32),
                ],
                axis=0,
            ).astype(BF)


def conv_call(lengths, x, g, lo, hi, w, proj, attn, log, q, k, v):
    chunk = lambda i, *_: (0, 0, i)
    flat = lambda i, *_: (0, i)
    full3 = lambda i, *_: (0, 0, 0)
    full2 = lambda i, *_: (0, 0)
    return pl.pallas_call(
        conv_kernel,
        out_shape=(
            sds((1, ROWS, 1024)),
            sds((8, 544, 128)),
            sds((HEADS, 400, 128)),
        ),
        grid_spec=pltpu.PrefetchScalarGridSpec(
            num_scalar_prefetch=1,
            grid=(1024 // WIDTH,),
            in_specs=[
                pl.BlockSpec((1, ROWS, WIDTH), chunk),
                pl.BlockSpec((1, ROWS, WIDTH), chunk),
                pl.BlockSpec((48, WIDTH), flat),
                pl.BlockSpec((48, WIDTH), flat),
                pl.BlockSpec((TAPS, WIDTH), flat),
                pl.BlockSpec((512, WIDTH), flat),
                pl.BlockSpec((1, ROWS, 512), full3),
                pl.BlockSpec((HEADS, ROWS), full2),
                pl.BlockSpec((1, ROWS, WIDTH // 2), chunk),
                pl.BlockSpec((1, ROWS, WIDTH // 2), chunk),
                pl.BlockSpec((1, ROWS, WIDTH // 2), chunk),
            ],
            out_specs=[
                pl.BlockSpec((1, ROWS, WIDTH), chunk),
                pl.BlockSpec((WIDTH // 128, 544, 128), lambda i, *_: (i, 0, 0)),
                pl.BlockSpec((HEADS, 400, 128), full3),
            ],
            scratch_shapes=[
                pltpu.VMEM((256, 128), F32),
                pltpu.VMEM((224, 128), F32),
                pltpu.VMEM((224, 128), F32),
                pltpu.VMEM((ROWS, 512), F32),
                pltpu.VMEM((512, ROWS), BF),
                pltpu.VMEM((256, 512), F32),
            ],
        ),
        compiler_params=pltpu.CompilerParams(vmem_limit_bytes=FREE << 20),
        cost_estimate=cost(11),
    )(lengths, x, g, lo, hi, w, proj, attn, log, q, k, v)


CHUNK = HEADS * ROWS
BU = 512


def key_rows(part, z, lanes):
    xh = lax.axis_index("xh")
    half = 1 - xh if part == 0 else xh
    row = ((half * 8 + z) * 2 + lax.axis_index("core")) * ROWS
    return row + lax.broadcasted_iota(jnp.int32, (ROWS, lanes), 0)


def unpack_rows(x, z, dst):
    left, right = x[:, 0:HSIZE], x[:, HSIZE:128]
    at, end = z * 128, 1024 + z * 64
    dst[at : at + 96, :] = left
    dst[at + 96 : at + 128, :] = right[0:32]
    dst[end : end + 64, :] = right[32:96]


def turn_rows(dqt, dq, put):
    for b in range(3):
        dq[b * 512 : b * 512 + 512, :] = dqt[:, b * 512 : b * 512 + 512].T
    for z in range(8):
        at, end = z * 128, 1024 + z * 64
        put(z, slice(0, 96), slice(0, HSIZE), dq[at : at + 96, :])
        put(z, slice(0, 32), slice(HSIZE, 128), dq[at + 96 : at + 128, :])
        put(z, slice(32, 96), slice(HSIZE, 128), dq[end : end + 64, :])


def prep_queries(x_ref, q_ref, do_ref, st_ref):
    lane = lax.broadcasted_iota(jnp.int32, (1, 128), 1)
    stats = []
    for z in range(8):
        unpack_rows(x_ref[z, 0:HALF, :], z, q_ref)
        unpack_rows(x_ref[z, HALF:ROWS, :], z, do_ref)
        st = x_ref[z, ROWS : ROWS + 16, :].astype(F32)
        st_ref[0:1, z * 128 : z * 128 + 128] = st[0:1]
        st_ref[1:2, z * 128 : z * 128 + 128] = st[2:3]
        stats.append(st)
    for m in range(4):
        a, b = stats[2 * m], stats[2 * m + 1]
        at = 1024 + m * 128
        for row in range(2):
            src = 2 * row + 1
            st_ref[row : row + 1, at : at + 128] = jnp.where(
                lane < 64, a[src : src + 1], pltpu.roll(b[src : src + 1], 64, 1)
            )


def prep_keys(part, lengths_ref, x_ref, k_ref, v_ref, kt_ref, kf):
    length = record_length(lengths_ref)
    for z in range(8):
        kv = x_ref[z]
        rows = slice(z * ROWS, z * ROWS + ROWS)
        k_ref[rows, :] = kv[:, 0:HSIZE]
        v_ref[rows, :] = kv[:, HSIZE:128]
        kf[rows, :] = jnp.where(key_rows(part, z, 128) < length, kv.astype(F32) * 0.125, 0.0)
    for b in range(3):
        turned = kf[b * 512 : b * 512 + 512, :].T
        kt_ref[:, b * 512 : b * 512 + 512] = turned[0:HSIZE].astype(BF)


def score_tile(q, do, st, k, v, kt, dqt, dks, dvs):
    def key_block(ui, _):
        u0 = pl.multiple_of(ui * BU, BU)
        kb = k[pl.ds(u0, BU), :]
        vb = v[pl.ds(u0, BU), :]
        ktb = kt[:, pl.ds(u0, BU)]
        qb, dob = q[...], do[...]
        s = lax.dot_general(kb, qb, NT, preferred_element_type=F32)
        p = jnp.exp(s - st[1:2, :])
        dp = lax.dot_general(vb, dob, NT, preferred_element_type=F32)
        ds = (p * (dp - st[0:1, :])).astype(BF)
        dvs[pl.ds(u0, BU), :] += lax.dot_general(p.astype(BF), dob, NN, preferred_element_type=F32)
        dks[pl.ds(u0, BU), :] += lax.dot_general(ds, qb, NN, preferred_element_type=F32)
        dqt[...] += lax.dot_general(ktb, ds, NN, preferred_element_type=F32)
        return 0

    lax.fori_loop(0, CHUNK // BU, key_block, 0)


def tile_1(q, do, st, k, v, kt, dqt, dks, dvs):
    for ref in (dqt, dks, dvs):
        ref[...] = jnp.zeros_like(ref)
    score_tile(q, do, st, k, v, kt, dqt, dks, dvs)


def pack_queries(dqt, dq, dq_ref):
    def put(z, rows, cols, value):
        dq_ref[z, rows, cols] = value.astype(BF)

    turn_rows(dqt, dq, put)


def pack_keys(part, lengths_ref, dks, dvs, dkv_ref):
    length = record_length(lengths_ref)
    for z in range(8):
        keep = key_rows(part, z, HSIZE) < length
        rows = slice(z * ROWS, z * ROWS + ROWS)
        dkv_ref[z, :, 0:HSIZE] = jnp.where(keep, dks[rows, :], 0.0).astype(BF)
        dkv_ref[z, :, HSIZE:128] = jnp.where(keep, dvs[rows, :], 0.0).astype(BF)


def tile_2(q, do, st, k, v, kt, dq_in, dq_ref, dks, dvs, dqt, dq):
    dqt[...] = dq_in[...]
    dks[...] = jnp.zeros_like(dks)
    dvs[...] = jnp.zeros_like(dvs)
    score_tile(q, do, st, k, v, kt, dqt, dks, dvs)
    pack_queries(dqt, dq, dq_ref)


def tile_3(lengths_ref, q, do, st, k, v, kt, dk_ref, dv_ref, dkv_ref, dqt, dks, dvs):
    dqt[...] = jnp.zeros_like(dqt)
    dks[...] = dk_ref[...]
    dvs[...] = dv_ref[...]
    score_tile(q, do, st, k, v, kt, dqt, dks, dvs)
    pack_keys(0, lengths_ref, dks, dvs, dkv_ref)


def tile_4(
    lengths_ref, q, do, st, k, v, kt, dq_in, dk_ref, dv_ref, dq_ref, dkv_ref, dks, dvs, dqt, dq
):
    dqt[...] = dq_in[...]
    dks[...] = dk_ref[...]
    dvs[...] = dv_ref[...]
    score_tile(q, do, st, k, v, kt, dqt, dks, dvs)
    pack_queries(dqt, dq, dq_ref)
    pack_keys(1, lengths_ref, dks, dvs, dkv_ref)


def tile_call(body, lengths, args, outs, scratch=()):
    whole = lambda x: pl.BlockSpec(x.shape, lambda *_: (0,) * len(x.shape))
    specs = [whole(a) for a in args]
    if lengths is not None:
        specs.insert(0, pl.BlockSpec(memory_space=pltpu.SMEM))
        args = (lengths,) + args
    return call(
        body,
        outs,
        7,
        40,
        grid=(1,),
        in_specs=specs,
        out_specs=tuple(whole(o) for o in outs),
        scratch_shapes=scratch,
    )(*args)


def combine(dkv_ref, dkv_got_ref, dq_ref, dq_got_ref, o_ref):
    o_ref[:, 0:ROWS, :] = (dkv_ref[...].astype(F32) + dkv_got_ref[...].astype(F32)).astype(BF)
    o_ref[:, ROWS:, :] = (dq_ref[...].astype(F32) + dq_got_ref[...].astype(F32)).astype(BF)


def unpack_final(x_ref, q_ref, k_ref, v_ref):
    for h in range(HEADS):
        cols = slice(h * HSIZE, (h + 1) * HSIZE)
        k_ref[0, :, cols] = x_ref[h, 0:ROWS, 0:HSIZE]
        v_ref[0, :, cols] = x_ref[h, 0:ROWS, HSIZE:128]
        q_ref[0, 0:HALF, cols] = x_ref[h, ROWS : ROWS + HALF, 0:HSIZE]
        q_ref[0, HALF:ROWS, cols] = x_ref[h, ROWS : ROWS + HALF, HSIZE:128]


def finish_sums(lengths_ref, own_ref, got_ref, proj_ref, taps_ref):
    total = lengths_ref[0]
    for r in range(1, 8):
        total = total + lengths_ref[r]
    scale = lax.rsqrt(jnp.full((1, 128), total, jnp.int32).astype(F32))
    core = lax.axis_index("core")
    for c in range(8):
        cols = slice(c * 128, c * 128 + 128)
        own, got = own_ref[c % 4].astype(F32), got_ref[c % 4].astype(F32)
        x = jnp.where(core == c // 4, own, got) * scale
        proj_ref[:, cols] = x[0:512]
        taps_ref[:, cols] = x[512:543]


def flip(x, axis, mask, size):
    return lax.ppermute(x, axis, [(i, i ^ mask) for i in range(size)])


def add(*terms):
    pair = [a.astype(F32) + b.astype(F32) for a, b in zip(terms[::2], terms[1::2])]
    return (pair[0] if len(pair) == 1 else pair[0] + pair[1]).astype(BF)


def reduce_dp(x, shift, count):
    me = (lax.axis_index("dp") >> shift) & (count - 1)
    pieces = x.reshape(count, x.shape[0] // count, 128)
    piece = lambda i: lax.dynamic_index_in_dim(pieces, i, 0, keepdims=False)
    got = [flip(piece(me ^ d), "dp", d << shift, 8) for d in range(1, count)]
    return add(piece(me), *got)


def sum_four(x, low, high, beside):
    got = [flip(x, ("xh", "z"), mask, 16) for mask in (low, high, low | high)]
    return add(after(x, beside), *got)


def gather_y(x, beside):
    y = lax.axis_index("dp") >> 1
    odd, upper = (y & 1) == 1, (y & 2) == 2
    b, c, d = [flip(x, "dp", m << 1, 8) for m in (1, 2, 3)]
    a = after(x, beside)
    low = jnp.concatenate([jnp.where(odd, b, a), jnp.where(odd, a, b)], axis=0)
    high = jnp.concatenate([jnp.where(odd, d, c), jnp.where(odd, c, d)], axis=0)
    return jnp.concatenate([jnp.where(upper, high, low), jnp.where(upper, low, high)], axis=0)


def gather_x(x, beside):
    odd = (lax.axis_index("dp") & 1) == 1
    got = flip(x, "dp", 1, 8)
    x = after(x, beside)
    return jnp.concatenate([jnp.where(odd, got, x), jnp.where(odd, x, got)], axis=0)


def after(x, *first):
    return lax.optimization_barrier((x,) + first)[0]


def swap(x, axis):
    return lax.ppermute(x, axis, [(0, 1), (1, 0)])


def shards(query, key, value, attn, log, lengths, x, g, proj, taps):
    smem = pl.BlockSpec(memory_space=pltpu.SMEM)
    vmem = pl.BlockSpec(memory_space=pltpu.VMEM)
    up = [(i, i + 1) for i in range(31)]
    down = [(i + 1, i) for i in range(31)]
    last, first = rims_call(x, g)
    lo = lax.ppermute(last, SEQ, up)
    hi = lax.ppermute(first, SEQ, down)
    grad_state, sums, pay = conv_call(
        lengths, x, g, lo, hi, taps, proj, attn, log[0].T, query, key, value
    )
    pay = lax.all_to_all(pay, "z", 0, 0, tiled=True)

    core = lax.axis_index("core")
    sums = sums.reshape(2, 2176, 128)
    send = lax.dynamic_index_in_dim(sums, 1 - core, 0, keepdims=False)
    keep = lax.dynamic_index_in_dim(sums, core, 0, keepdims=False)
    sums = add(keep, swap(send, "core"))
    sums = reduce_dp(sums, 0, 2)
    sums = reduce_dp(sums, 1, 4)

    queries, keys = pay[:, ROWS:], pay[:, :ROWS]
    core_queries, other_keys = swap(queries, "core"), swap(keys, "xh")

    half = sds((CHUNK, HSIZE))

    def prepared_queries(x):
        return call(prep_queries, (half, half, sds((8, CHUNK), F32)), 1, 8)(x)

    def prepared_keys(part, x):
        return call(
            functools.partial(prep_keys, part),
            (half, half, sds((HSIZE, CHUNK))),
            1,
            8,
            in_specs=[smem, vmem],
            scratch_shapes=[pltpu.VMEM((CHUNK, 128), F32)],
        )(lengths, x)

    qo = prepared_queries(queries)
    ko = prepared_keys(1, keys)
    grad = sds((CHUNK, HSIZE), F32)
    turned = sds((HSIZE, CHUNK), F32)
    fgrad = pltpu.VMEM((CHUNK, HSIZE), F32)
    fturned = pltpu.VMEM((HSIZE, CHUNK), F32)
    dqo, dk, dv = tile_call(tile_1, None, qo + ko, (turned, grad, grad))
    sums = sum_four(sums, 1, 8, dk)

    kx = prepared_keys(0, other_keys)
    dqo = after(dqo, sums)
    packed_q = sds((8, HALF, 128))
    packed_k = sds((HEADS, ROWS, 128))
    dqo, dkx, dvx = tile_call(
        tile_2, None, qo + kx + (dqo,), (packed_q, grad, grad), [fturned, fgrad]
    )
    sums = sum_four(sums, 2, 4, dvx)

    qc = prepared_queries(core_queries)
    dkx = after(dkx, sums)
    dkv_other, dqc = tile_call(
        tile_3, lengths, qc + kx + (dkx, dvx), (packed_k, turned), [fgrad, fgrad]
    )
    dkv_got = swap(dkv_other, "xh")
    sums = gather_y(sums, dqc)
    dqc = after(dqc, sums)
    dq_core, dkv_own = tile_call(
        tile_4,
        lengths,
        qc + ko + (dqc, dk, dv),
        (packed_q, packed_k),
        [fgrad, fgrad, fturned, fgrad],
    )
    dq_got = swap(dq_core, "core")
    back = call(
        combine, sds((HEADS, ROWS + HALF, 128)), 1, 8, in_specs=[vmem] * 4
    )(dkv_own, dkv_got, dqo, dq_got)

    sums = gather_x(sums, back)
    back = lax.all_to_all(back, "z", 0, 0, tiled=True)
    sums = sums.reshape(4, 544, 128)
    grad_proj, grad_taps = call(
        finish_sums,
        (sds((512, 1024), F32), sds((TAPS, 1024), F32)),
        2,
        8,
        in_specs=[smem, vmem, vmem],
    )(lengths, sums, swap(sums, "core"))
    grad_q, grad_k, grad_v = call(unpack_final, (sds((1, ROWS, 512)),) * 3, 2, 8)(back)
    return grad_q, grad_k, grad_v, grad_state, grad_proj, grad_taps


def solution(mesh):
    inner = Mesh(mesh.devices.reshape(8, 2, 8, 2), ALL)
    rows = P("dp", SEQ, None)
    in_specs = (rows,) * 5 + (P(), rows, rows, P(), P())
    out_specs = (rows,) * 4 + (P(), P())
    return jax.shard_map(
        shards, mesh=inner, in_specs=in_specs, out_specs=out_specs, check_vma=False
    )
```

```python
import functools

import jax
import jax.numpy as jnp
from jax import lax
from jax.experimental import pallas as pl
from jax.experimental.pallas import tpu as pltpu
from jax.sharding import Mesh, PartitionSpec as P

BF = jnp.bfloat16
F32 = jnp.float32
NT = (((1,), (1,)), ((), ()))
NN = (((1,), (0,)), ((), ()))
TN = (((0,), (0,)), ((), ()))
ROWS = 192
HALF = 96
HEADS = 8
HSIZE = 64
TAPS = 31
FREE = 60
WIDTH = 512
ALL = ("dp", "xh", "z", "core")
SEQ = ("xh", "z", "core")


def cost(micros):
    return pl.CostEstimate(flops=int(micros * 1.15e9), transcendentals=0, bytes_accessed=1 << 20)


def call(kernel, out_shape, micros, vmem, **kw):
    return pl.pallas_call(
        kernel,
        out_shape=out_shape,
        compiler_params=pltpu.CompilerParams(vmem_limit_bytes=vmem << 20),
        cost_estimate=cost(micros),
        **kw,
    )


def record_length(lengths_ref):
    return lengths_ref[lax.axis_index("dp")]


def sds(shape, dtype=BF):
    return jax.ShapeDtypeStruct(shape, dtype)


def rims(xl_ref, xf_ref, gl_ref, gf_ref, last_ref, first_ref):
    last_ref[0:32, :] = xl_ref[0]
    last_ref[32:48, :] = gl_ref[0]
    first_ref[0:32, :] = xf_ref[0]
    first_ref[32:48, :] = gf_ref[0]


def rims_call(x, g):
    rim = lambda n, at: pl.BlockSpec((1, n, 1024), lambda i: (0, at, 0))
    edge = pl.BlockSpec((48, 1024), lambda i: (0, 0))
    return call(
        rims,
        (sds((48, 1024)), sds((48, 1024))),
        1,
        FREE,
        grid=(1,),
        in_specs=[rim(32, 5), rim(32, 0), rim(16, 11), rim(16, 0)],
        out_specs=[edge, edge],
    )(x, x, g, g)


def conv_kernel(
    lengths_ref,
    x_ref,
    g_ref,
    lo_ref,
    hi_ref,
    w_ref,
    proj_ref,
    attn_ref,
    log_ref,
    q_ref,
    k_ref,
    v_ref,
    gs_ref,
    pk_ref,
    pay_ref,
    xs,
    gm,
    gp,
    out_acc,
    attn_t,
    tmp,
):
    step = pl.program_id(0)
    first_row = lax.axis_index(SEQ) * ROWS
    length = record_length(lengths_ref)

    @pl.when(step == 0)
    def _():
        out_acc[...] = jnp.zeros_like(out_acc)
        attn_t[...] = attn_ref[0].T

    heads = WIDTH // 128
    for i in range(heads):
        cols = slice(i * HSIZE, (i + 1) * HSIZE)
        h = pl.ds(heads * step + i, 1)
        pay_ref[h, 0:ROWS, 0:HSIZE] = k_ref[:, :, cols]
        pay_ref[h, 0:ROWS, HSIZE:128] = v_ref[:, :, cols]
        q = q_ref[:, :, cols] * BF(0.125)
        pay_ref[h, ROWS : ROWS + HALF, 0:HSIZE] = q[:, :HALF]
        pay_ref[h, ROWS : ROWS + HALF, HSIZE:128] = q[:, HALF:]

    def mask(rows, offset):
        at = first_row + offset + lax.broadcasted_iota(jnp.int32, (rows, 128), 0)
        return jnp.where((at >= 0) & (at < length), 1.0, 0.0).astype(F32)

    mask_x = mask(256, -32)
    mask_g = mask(224, -16)
    for half in range(WIDTH // 128):
        cols = slice(half * 128, half * 128 + 128)
        xs[0:32, :] = lo_ref[0:32, cols].astype(F32) * mask_x[0:32]
        xs[32:224, :] = x_ref[0, :, cols].astype(F32) * mask_x[32:224]
        xs[224:256, :] = hi_ref[0:32, cols].astype(F32) * mask_x[224:256]
        gm[0:16, :] = lo_ref[32:48, cols].astype(F32) * mask_g[0:16]
        gm[16:208, :] = g_ref[0, :, cols].astype(F32) * mask_g[16:208]
        gm[208:224, :] = hi_ref[32:48, cols].astype(F32) * mask_g[208:224]
        pre = jnp.zeros((224, 128), F32)
        for j in range(TAPS):
            pre = pre + w_ref[j : j + 1, cols] * xs[1 + j : 225 + j, :]
        s = jax.nn.sigmoid(pre)
        gp[...] = (gm[...] * s * (1.0 + pre * (1.0 - s))).astype(BF).astype(F32)
        back = jnp.zeros((ROWS, 128), F32)
        for j in range(TAPS):
            back = back + w_ref[j : j + 1, cols] * gp[31 - j : 223 - j, :]
        gs = (gm[16:208, :] + mask_g[16:208] * back).astype(BF)
        gs_ref[0, :, cols] = gs
        out_acc[...] += lax.dot_general(
            gs, proj_ref[:, cols], NT, preferred_element_type=F32
        )
        pk_ref[half, 0:512, :] = lax.dot_general(
            attn_t[...], gs, NN, preferred_element_type=F32
        ).astype(BF)
        own = gp[16:208, :]
        rows = [
            jnp.sum(xs[17 + j : 209 + j, :] * own, axis=0, keepdims=True) for j in range(TAPS)
        ]
        rows.append(jnp.zeros((1, 128), F32))
        pk_ref[half, 512:544, :] = jnp.concatenate(rows, axis=0).astype(BF)

    @pl.when(step == pl.num_programs(0) - 1)
    def _():
        grad = out_acc[...].astype(BF)
        tmp[0:ROWS, :] = grad.astype(F32) * attn_ref[0].astype(F32)
        tmp[ROWS:256, :] = jnp.zeros((256 - ROWS, 512), F32)
        turned = tmp[...].T
        logs = jnp.concatenate(
            [log_ref[...].astype(F32), jnp.zeros((HEADS, 256 - ROWS), F32)], axis=1
        )
        for h in range(HEADS):
            delta = jnp.sum(turned[h * HSIZE : (h + 1) * HSIZE], axis=0, keepdims=True)
            log_row = logs[h : h + 1]
            part = grad[:, h * HSIZE : (h + 1) * HSIZE]
            pay_ref[h, 288:384, 0:HSIZE] = part[:HALF]
            pay_ref[h, 288:384, HSIZE:128] = part[HALF:]
            pay_ref[h, 384:400, :] = jnp.concatenate(
                [
                    delta[:, 0:128],
                    delta[:, 128:256],
                    log_row[:, 0:128],
                    log_row[:, 128:256],
                    jnp.zeros((12, 128), F32),
                ],
                axis=0,
            ).astype(BF)


def conv_call(lengths, x, g, lo, hi, w, proj, attn, log, q, k, v):
    chunk = lambda i, *_: (0, 0, i)
    flat = lambda i, *_: (0, i)
    full3 = lambda i, *_: (0, 0, 0)
    full2 = lambda i, *_: (0, 0)
    return pl.pallas_call(
        conv_kernel,
        out_shape=(
            sds((1, ROWS, 1024)),
            sds((8, 544, 128)),
            sds((HEADS, 400, 128)),
        ),
        grid_spec=pltpu.PrefetchScalarGridSpec(
            num_scalar_prefetch=1,
            grid=(1024 // WIDTH,),
            in_specs=[
                pl.BlockSpec((1, ROWS, WIDTH), chunk),
                pl.BlockSpec((1, ROWS, WIDTH), chunk),
                pl.BlockSpec((48, WIDTH), flat),
                pl.BlockSpec((48, WIDTH), flat),
                pl.BlockSpec((TAPS, WIDTH), flat),
                pl.BlockSpec((512, WIDTH), flat),
                pl.BlockSpec((1, ROWS, 512), full3),
                pl.BlockSpec((HEADS, ROWS), full2),
                pl.BlockSpec((1, ROWS, WIDTH // 2), chunk),
                pl.BlockSpec((1, ROWS, WIDTH // 2), chunk),
                pl.BlockSpec((1, ROWS, WIDTH // 2), chunk),
            ],
            out_specs=[
                pl.BlockSpec((1, ROWS, WIDTH), chunk),
                pl.BlockSpec((WIDTH // 128, 544, 128), lambda i, *_: (i, 0, 0)),
                pl.BlockSpec((HEADS, 400, 128), full3),
            ],
            scratch_shapes=[
                pltpu.VMEM((256, 128), F32),
                pltpu.VMEM((224, 128), F32),
                pltpu.VMEM((224, 128), F32),
                pltpu.VMEM((ROWS, 512), F32),
                pltpu.VMEM((512, ROWS), BF),
                pltpu.VMEM((256, 512), F32),
            ],
        ),
        compiler_params=pltpu.CompilerParams(vmem_limit_bytes=FREE << 20),
        cost_estimate=cost(11),
    )(lengths, x, g, lo, hi, w, proj, attn, log, q, k, v)


CHUNK = HEADS * ROWS
BU = 512


def key_rows(part, z, lanes):
    xh = lax.axis_index("xh")
    half = 1 - xh if part == 0 else xh
    row = ((half * 8 + z) * 2 + lax.axis_index("core")) * ROWS
    return row + lax.broadcasted_iota(jnp.int32, (ROWS, lanes), 0)


def unpack_rows(x, z, dst):
    left, right = x[:, 0:HSIZE], x[:, HSIZE:128]
    at, end = z * 128, 1024 + z * 64
    dst[at : at + 96, :] = left
    dst[at + 96 : at + 128, :] = right[0:32]
    dst[end : end + 64, :] = right[32:96]


def turn_rows(dqt, dq, put):
    for b in range(3):
        dq[b * 512 : b * 512 + 512, :] = dqt[:, b * 512 : b * 512 + 512].T
    for z in range(8):
        at, end = z * 128, 1024 + z * 64
        put(z, slice(0, 96), slice(0, HSIZE), dq[at : at + 96, :])
        put(z, slice(0, 32), slice(HSIZE, 128), dq[at + 96 : at + 128, :])
        put(z, slice(32, 96), slice(HSIZE, 128), dq[end : end + 64, :])


def prep_queries(x_ref, q_ref, do_ref, st_ref):
    lane = lax.broadcasted_iota(jnp.int32, (1, 128), 1)
    stats = []
    for z in range(8):
        unpack_rows(x_ref[z, 0:HALF, :], z, q_ref)
        unpack_rows(x_ref[z, HALF:ROWS, :], z, do_ref)
        st = x_ref[z, ROWS : ROWS + 16, :].astype(F32)
        st_ref[0:1, z * 128 : z * 128 + 128] = st[0:1]
        st_ref[1:2, z * 128 : z * 128 + 128] = st[2:3]
        stats.append(st)
    for m in range(4):
        a, b = stats[2 * m], stats[2 * m + 1]
        at = 1024 + m * 128
        for row in range(2):
            src = 2 * row + 1
            st_ref[row : row + 1, at : at + 128] = jnp.where(
                lane < 64, a[src : src + 1], pltpu.roll(b[src : src + 1], 64, 1)
            )


def prep_keys(part, lengths_ref, x_ref, k_ref, v_ref, kt_ref, kf):
    length = record_length(lengths_ref)
    for z in range(8):
        kv = x_ref[z]
        rows = slice(z * ROWS, z * ROWS + ROWS)
        k_ref[rows, :] = kv[:, 0:HSIZE]
        v_ref[rows, :] = kv[:, HSIZE:128]
        kf[rows, :] = jnp.where(key_rows(part, z, 128) < length, kv.astype(F32) * 0.125, 0.0)
    for b in range(3):
        turned = kf[b * 512 : b * 512 + 512, :].T
        kt_ref[:, b * 512 : b * 512 + 512] = turned[0:HSIZE].astype(BF)


def score_tile(q, do, st, k, v, kt, dqt, dks, dvs):
    def key_block(ui, _):
        u0 = pl.multiple_of(ui * BU, BU)
        kb = k[pl.ds(u0, BU), :]
        vb = v[pl.ds(u0, BU), :]
        ktb = kt[:, pl.ds(u0, BU)]
        qb, dob = q[...], do[...]
        s = lax.dot_general(kb, qb, NT, preferred_element_type=F32)
        p = jnp.exp(s - st[1:2, :])
        dp = lax.dot_general(vb, dob, NT, preferred_element_type=F32)
        ds = (p * (dp - st[0:1, :])).astype(BF)
        dvs[pl.ds(u0, BU), :] += lax.dot_general(p.astype(BF), dob, NN, preferred_element_type=F32)
        dks[pl.ds(u0, BU), :] += lax.dot_general(ds, qb, NN, preferred_element_type=F32)
        dqt[...] += lax.dot_general(ktb, ds, NN, preferred_element_type=F32)
        return 0

    lax.fori_loop(0, CHUNK // BU, key_block, 0)


def tile_1(q, do, st, k, v, kt, dqt, dks, dvs):
    for ref in (dqt, dks, dvs):
        ref[...] = jnp.zeros_like(ref)
    score_tile(q, do, st, k, v, kt, dqt, dks, dvs)


def pack_queries(dqt, dq, dq_ref):
    def put(z, rows, cols, value):
        dq_ref[z, rows, cols] = value.astype(BF)

    turn_rows(dqt, dq, put)


def pack_keys(part, lengths_ref, dks, dvs, dkv_ref):
    length = record_length(lengths_ref)
    for z in range(8):
        keep = key_rows(part, z, HSIZE) < length
        rows = slice(z * ROWS, z * ROWS + ROWS)
        dkv_ref[z, :, 0:HSIZE] = jnp.where(keep, dks[rows, :], 0.0).astype(BF)
        dkv_ref[z, :, HSIZE:128] = jnp.where(keep, dvs[rows, :], 0.0).astype(BF)


def tile_2(q, do, st, k, v, kt, dq_in, dq_ref, dks, dvs, dqt, dq):
    dqt[...] = dq_in[...]
    dks[...] = jnp.zeros_like(dks)
    dvs[...] = jnp.zeros_like(dvs)
    score_tile(q, do, st, k, v, kt, dqt, dks, dvs)
    pack_queries(dqt, dq, dq_ref)


def tile_3(lengths_ref, q, do, st, k, v, kt, dk_ref, dv_ref, dkv_ref, dqt, dks, dvs):
    dqt[...] = jnp.zeros_like(dqt)
    dks[...] = dk_ref[...]
    dvs[...] = dv_ref[...]
    score_tile(q, do, st, k, v, kt, dqt, dks, dvs)
    pack_keys(0, lengths_ref, dks, dvs, dkv_ref)


def tile_4(
    lengths_ref, q, do, st, k, v, kt, dq_in, dk_ref, dv_ref, dq_ref, dkv_ref, dks, dvs, dqt, dq
):
    dqt[...] = dq_in[...]
    dks[...] = dk_ref[...]
    dvs[...] = dv_ref[...]
    score_tile(q, do, st, k, v, kt, dqt, dks, dvs)
    pack_queries(dqt, dq, dq_ref)
    pack_keys(1, lengths_ref, dks, dvs, dkv_ref)


def tile_call(body, lengths, args, outs, scratch=()):
    whole = lambda x: pl.BlockSpec(x.shape, lambda *_: (0,) * len(x.shape))
    specs = [whole(a) for a in args]
    if lengths is not None:
        specs.insert(0, pl.BlockSpec(memory_space=pltpu.SMEM))
        args = (lengths,) + args
    return call(
        body,
        outs,
        7,
        40,
        grid=(1,),
        in_specs=specs,
        out_specs=tuple(whole(o) for o in outs),
        scratch_shapes=scratch,
    )(*args)


def combine(dkv_ref, dkv_got_ref, dq_ref, dq_got_ref, o_ref):
    o_ref[:, 0:ROWS, :] = (dkv_ref[...].astype(F32) + dkv_got_ref[...].astype(F32)).astype(BF)
    o_ref[:, ROWS:, :] = (dq_ref[...].astype(F32) + dq_got_ref[...].astype(F32)).astype(BF)


def unpack_final(x_ref, q_ref, k_ref, v_ref):
    for h in range(HEADS):
        cols = slice(h * HSIZE, (h + 1) * HSIZE)
        k_ref[0, :, cols] = x_ref[h, 0:ROWS, 0:HSIZE]
        v_ref[0, :, cols] = x_ref[h, 0:ROWS, HSIZE:128]
        q_ref[0, 0:HALF, cols] = x_ref[h, ROWS : ROWS + HALF, 0:HSIZE]
        q_ref[0, HALF:ROWS, cols] = x_ref[h, ROWS : ROWS + HALF, HSIZE:128]


def finish_sums(lengths_ref, own_ref, got_ref, proj_ref, taps_ref):
    total = lengths_ref[0]
    for r in range(1, 8):
        total = total + lengths_ref[r]
    scale = lax.rsqrt(jnp.full((1, 128), total, jnp.int32).astype(F32))
    core = lax.axis_index("core")
    for c in range(8):
        cols = slice(c * 128, c * 128 + 128)
        own, got = own_ref[c % 4].astype(F32), got_ref[c % 4].astype(F32)
        x = jnp.where(core == c // 4, own, got) * scale
        proj_ref[:, cols] = x[0:512]
        taps_ref[:, cols] = x[512:543]


def flip(x, axis, mask, size):
    return lax.ppermute(x, axis, [(i, i ^ mask) for i in range(size)])


def add(*terms):
    pair = [a.astype(F32) + b.astype(F32) for a, b in zip(terms[::2], terms[1::2])]
    return (pair[0] if len(pair) == 1 else pair[0] + pair[1]).astype(BF)


def reduce_dp(x, shift, count):
    me = (lax.axis_index("dp") >> shift) & (count - 1)
    pieces = x.reshape(count, x.shape[0] // count, 128)
    piece = lambda i: lax.dynamic_index_in_dim(pieces, i, 0, keepdims=False)
    got = [flip(piece(me ^ d), "dp", d << shift, 8) for d in range(1, count)]
    return add(piece(me), *got)


def sum_four(x, low, high, beside):
    got = [flip(x, ("xh", "z"), mask, 16) for mask in (low, high, low | high)]
    return add(after(x, beside), *got)


def sum_two(x, mask, beside):
    return add(after(x, beside), flip(x, ("xh", "z"), mask, 16))


def gather_y(x, beside):
    y = lax.axis_index("dp") >> 1
    odd, upper = (y & 1) == 1, (y & 2) == 2
    b, c, d = [flip(x, "dp", m << 1, 8) for m in (1, 2, 3)]
    a = after(x, beside)
    low = jnp.concatenate([jnp.where(odd, b, a), jnp.where(odd, a, b)], axis=0)
    high = jnp.concatenate([jnp.where(odd, d, c), jnp.where(odd, c, d)], axis=0)
    return jnp.concatenate([jnp.where(upper, high, low), jnp.where(upper, low, high)], axis=0)


def gather_x(x, beside):
    odd = (lax.axis_index("dp") & 1) == 1
    got = flip(x, "dp", 1, 8)
    x = after(x, beside)
    return jnp.concatenate([jnp.where(odd, got, x), jnp.where(odd, x, got)], axis=0)


def after(x, *first):
    return lax.optimization_barrier((x,) + first)[0]


def swap(x, axis):
    return lax.ppermute(x, axis, [(0, 1), (1, 0)])


def shards(query, key, value, attn, log, lengths, x, g, proj, taps):
    smem = pl.BlockSpec(memory_space=pltpu.SMEM)
    vmem = pl.BlockSpec(memory_space=pltpu.VMEM)
    up = [(i, i + 1) for i in range(31)]
    down = [(i + 1, i) for i in range(31)]
    last, first = rims_call(x, g)
    lo = lax.ppermute(last, SEQ, up)
    hi = lax.ppermute(first, SEQ, down)
    grad_state, sums, pay = conv_call(
        lengths, x, g, lo, hi, taps, proj, attn, log[0].T, query, key, value
    )
    pay = lax.all_to_all(pay, "z", 0, 0, tiled=True)

    core = lax.axis_index("core")
    sums = sums.reshape(2, 2176, 128)
    send = lax.dynamic_index_in_dim(sums, 1 - core, 0, keepdims=False)
    keep = lax.dynamic_index_in_dim(sums, core, 0, keepdims=False)
    sums = add(keep, swap(send, "core"))
    sums = reduce_dp(sums, 0, 2)
    sums = reduce_dp(sums, 1, 4)

    queries, keys = pay[:, ROWS:], pay[:, :ROWS]
    core_queries, other_keys = swap(queries, "core"), swap(keys, "xh")

    half = sds((CHUNK, HSIZE))

    def prepared_queries(x):
        return call(prep_queries, (half, half, sds((8, CHUNK), F32)), 1, 8)(x)

    def prepared_keys(part, x):
        return call(
            functools.partial(prep_keys, part),
            (half, half, sds((HSIZE, CHUNK))),
            1,
            8,
            in_specs=[smem, vmem],
            scratch_shapes=[pltpu.VMEM((CHUNK, 128), F32)],
        )(lengths, x)

    qo = prepared_queries(queries)
    ko = prepared_keys(1, keys)
    grad = sds((CHUNK, HSIZE), F32)
    turned = sds((HSIZE, CHUNK), F32)
    fgrad = pltpu.VMEM((CHUNK, HSIZE), F32)
    fturned = pltpu.VMEM((HSIZE, CHUNK), F32)
    dqo, dk, dv = tile_call(tile_1, None, qo + ko, (turned, grad, grad))
    sums = sum_four(sums, 1, 8, dk)

    kx = prepared_keys(0, other_keys)
    dqo = after(dqo, sums)
    packed_q = sds((8, HALF, 128))
    packed_k = sds((HEADS, ROWS, 128))
    dqo, dkx, dvx = tile_call(
        tile_2, None, qo + kx + (dqo,), (packed_q, grad, grad), [fturned, fgrad]
    )
    sums = sum_two(sums, 2, dvx)

    qc = prepared_queries(core_queries)
    dkx = after(dkx, sums)
    dkv_other, dqc = tile_call(
        tile_3, lengths, qc + kx + (dkx, dvx), (packed_k, turned), [fgrad, fgrad]
    )
    dkv_got = swap(dkv_other, "xh")
    sums = sum_two(sums, 4, dqc)
    dqc = after(dqc, sums)
    dq_core, dkv_own = tile_call(
        tile_4,
        lengths,
        qc + ko + (dqc, dk, dv),
        (packed_q, packed_k),
        [fgrad, fgrad, fturned, fgrad],
    )
    dq_got = swap(dq_core, "core")
    back = call(
        combine, sds((HEADS, ROWS + HALF, 128)), 1, 8, in_specs=[vmem] * 4
    )(dkv_own, dkv_got, dqo, dq_got)

    sums = gather_x(gather_y(sums, dkv_own), back)
    back = lax.all_to_all(back, "z", 0, 0, tiled=True)
    sums = sums.reshape(4, 544, 128)
    grad_proj, grad_taps = call(
        finish_sums,
        (sds((512, 1024), F32), sds((TAPS, 1024), F32)),
        2,
        8,
        in_specs=[smem, vmem, vmem],
    )(lengths, sums, swap(sums, "core"))
    grad_q, grad_k, grad_v = call(unpack_final, (sds((1, ROWS, 512)),) * 3, 2, 8)(back)
    return grad_q, grad_k, grad_v, grad_state, grad_proj, grad_taps


def solution(mesh):
    inner = Mesh(mesh.devices.reshape(8, 2, 8, 2), ALL)
    rows = P("dp", SEQ, None)
    in_specs = (rows,) * 5 + (P(), rows, rows, P(), P())
    out_specs = (rows,) * 4 + (P(), P())
    return jax.shard_map(
        shards, mesh=inner, in_specs=in_specs, out_specs=out_specs, check_vma=False
    )
```

```python
import functools

import jax
import jax.numpy as jnp
from jax import lax
from jax.experimental import pallas as pl
from jax.experimental.pallas import tpu as pltpu
from jax.sharding import Mesh, PartitionSpec as P

BF = jnp.bfloat16
F32 = jnp.float32
NT = (((1,), (1,)), ((), ()))
NN = (((1,), (0,)), ((), ()))
TN = (((0,), (0,)), ((), ()))
ROWS = 192
HALF = 96
HEADS = 8
HSIZE = 64
TAPS = 31
FREE = 60
WIDTH = 1024
ALL = ("dp", "xh", "z", "core")
SEQ = ("xh", "z", "core")


def cost(micros):
    return pl.CostEstimate(flops=int(micros * 1.15e9), transcendentals=0, bytes_accessed=1 << 20)


def call(kernel, out_shape, micros, vmem, **kw):
    return pl.pallas_call(
        kernel,
        out_shape=out_shape,
        compiler_params=pltpu.CompilerParams(vmem_limit_bytes=vmem << 20),
        cost_estimate=cost(micros),
        **kw,
    )


def record_length(lengths_ref):
    return lengths_ref[lax.axis_index("dp")]


def sds(shape, dtype=BF):
    return jax.ShapeDtypeStruct(shape, dtype)


def rims(xl_ref, xf_ref, gl_ref, gf_ref, last_ref, first_ref):
    last_ref[0:32, :] = xl_ref[0]
    last_ref[32:48, :] = gl_ref[0]
    first_ref[0:32, :] = xf_ref[0]
    first_ref[32:48, :] = gf_ref[0]


def rims_call(x, g):
    rim = lambda n, at: pl.BlockSpec((1, n, 1024), lambda i: (0, at, 0))
    edge = pl.BlockSpec((48, 1024), lambda i: (0, 0))
    return call(
        rims,
        (sds((48, 1024)), sds((48, 1024))),
        1,
        FREE,
        grid=(1,),
        in_specs=[rim(32, 5), rim(32, 0), rim(16, 11), rim(16, 0)],
        out_specs=[edge, edge],
    )(x, x, g, g)


def conv_kernel(
    lengths_ref,
    x_ref,
    g_ref,
    lo_ref,
    hi_ref,
    w_ref,
    proj_ref,
    attn_ref,
    log_ref,
    q_ref,
    k_ref,
    v_ref,
    gs_ref,
    pk_ref,
    pay_ref,
    xs,
    gm,
    gp,
    out_acc,
    attn_t,
    tmp,
):
    step = pl.program_id(0)
    first_row = lax.axis_index(SEQ) * ROWS
    length = record_length(lengths_ref)

    @pl.when(step == 0)
    def _():
        out_acc[...] = jnp.zeros_like(out_acc)
        attn_t[...] = attn_ref[0].T

    heads = WIDTH // 128
    for i in range(heads):
        cols = slice(i * HSIZE, (i + 1) * HSIZE)
        h = pl.ds(heads * step + i, 1)
        pay_ref[h, 0:ROWS, 0:HSIZE] = k_ref[:, :, cols]
        pay_ref[h, 0:ROWS, HSIZE:128] = v_ref[:, :, cols]
        q = q_ref[:, :, cols] * BF(0.125)
        pay_ref[h, ROWS : ROWS + HALF, 0:HSIZE] = q[:, :HALF]
        pay_ref[h, ROWS : ROWS + HALF, HSIZE:128] = q[:, HALF:]

    def mask(rows, offset):
        at = first_row + offset + lax.broadcasted_iota(jnp.int32, (rows, 128), 0)
        return jnp.where((at >= 0) & (at < length), 1.0, 0.0).astype(F32)

    mask_x = mask(256, -32)
    mask_g = mask(224, -16)
    for half in range(WIDTH // 128):
        cols = slice(half * 128, half * 128 + 128)
        xs[0:32, :] = lo_ref[0:32, cols].astype(F32) * mask_x[0:32]
        xs[32:224, :] = x_ref[0, :, cols].astype(F32) * mask_x[32:224]
        xs[224:256, :] = hi_ref[0:32, cols].astype(F32) * mask_x[224:256]
        gm[0:16, :] = lo_ref[32:48, cols].astype(F32) * mask_g[0:16]
        gm[16:208, :] = g_ref[0, :, cols].astype(F32) * mask_g[16:208]
        gm[208:224, :] = hi_ref[32:48, cols].astype(F32) * mask_g[208:224]
        pre = jnp.zeros((224, 128), F32)
        for j in range(TAPS):
            pre = pre + w_ref[j : j + 1, cols] * xs[1 + j : 225 + j, :]
        s = jax.nn.sigmoid(pre)
        gp[...] = (gm[...] * s * (1.0 + pre * (1.0 - s))).astype(BF).astype(F32)
        back = jnp.zeros((ROWS, 128), F32)
        for j in range(TAPS):
            back = back + w_ref[j : j + 1, cols] * gp[31 - j : 223 - j, :]
        gs = (gm[16:208, :] + mask_g[16:208] * back).astype(BF)
        gs_ref[0, :, cols] = gs
        out_acc[...] += lax.dot_general(
            gs, proj_ref[:, cols], NT, preferred_element_type=F32
        )
        pk_ref[half, 0:512, :] = lax.dot_general(
            attn_t[...], gs, NN, preferred_element_type=F32
        ).astype(BF)
        own = gp[16:208, :]
        rows = [
            jnp.sum(xs[17 + j : 209 + j, :] * own, axis=0, keepdims=True) for j in range(TAPS)
        ]
        rows.append(jnp.zeros((1, 128), F32))
        pk_ref[half, 512:544, :] = jnp.concatenate(rows, axis=0).astype(BF)

    @pl.when(step == pl.num_programs(0) - 1)
    def _():
        grad = out_acc[...].astype(BF)
        tmp[0:ROWS, :] = grad.astype(F32) * attn_ref[0].astype(F32)
        tmp[ROWS:256, :] = jnp.zeros((256 - ROWS, 512), F32)
        turned = tmp[...].T
        logs = jnp.concatenate(
            [log_ref[...].astype(F32), jnp.zeros((HEADS, 256 - ROWS), F32)], axis=1
        )
        for h in range(HEADS):
            delta = jnp.sum(turned[h * HSIZE : (h + 1) * HSIZE], axis=0, keepdims=True)
            log_row = logs[h : h + 1]
            part = grad[:, h * HSIZE : (h + 1) * HSIZE]
            pay_ref[h, 288:384, 0:HSIZE] = part[:HALF]
            pay_ref[h, 288:384, HSIZE:128] = part[HALF:]
            pay_ref[h, 384:400, :] = jnp.concatenate(
                [
                    delta[:, 0:128],
                    delta[:, 128:256],
                    log_row[:, 0:128],
                    log_row[:, 128:256],
                    jnp.zeros((12, 128), F32),
                ],
                axis=0,
            ).astype(BF)


def conv_call(lengths, x, g, lo, hi, w, proj, attn, log, q, k, v):
    chunk = lambda i, *_: (0, 0, i)
    flat = lambda i, *_: (0, i)
    full3 = lambda i, *_: (0, 0, 0)
    full2 = lambda i, *_: (0, 0)
    return pl.pallas_call(
        conv_kernel,
        out_shape=(
            sds((1, ROWS, 1024)),
            sds((8, 544, 128)),
            sds((HEADS, 400, 128)),
        ),
        grid_spec=pltpu.PrefetchScalarGridSpec(
            num_scalar_prefetch=1,
            grid=(1024 // WIDTH,),
            in_specs=[
                pl.BlockSpec((1, ROWS, WIDTH), chunk),
                pl.BlockSpec((1, ROWS, WIDTH), chunk),
                pl.BlockSpec((48, WIDTH), flat),
                pl.BlockSpec((48, WIDTH), flat),
                pl.BlockSpec((TAPS, WIDTH), flat),
                pl.BlockSpec((512, WIDTH), flat),
                pl.BlockSpec((1, ROWS, 512), full3),
                pl.BlockSpec((HEADS, ROWS), full2),
                pl.BlockSpec((1, ROWS, WIDTH // 2), chunk),
                pl.BlockSpec((1, ROWS, WIDTH // 2), chunk),
                pl.BlockSpec((1, ROWS, WIDTH // 2), chunk),
            ],
            out_specs=[
                pl.BlockSpec((1, ROWS, WIDTH), chunk),
                pl.BlockSpec((WIDTH // 128, 544, 128), lambda i, *_: (i, 0, 0)),
                pl.BlockSpec((HEADS, 400, 128), full3),
            ],
            scratch_shapes=[
                pltpu.VMEM((256, 128), F32),
                pltpu.VMEM((224, 128), F32),
                pltpu.VMEM((224, 128), F32),
                pltpu.VMEM((ROWS, 512), F32),
                pltpu.VMEM((512, ROWS), BF),
                pltpu.VMEM((256, 512), F32),
            ],
        ),
        compiler_params=pltpu.CompilerParams(vmem_limit_bytes=FREE << 20),
        cost_estimate=cost(11),
    )(lengths, x, g, lo, hi, w, proj, attn, log, q, k, v)


CHUNK = HEADS * ROWS
BU = 512


def key_rows(part, z, lanes):
    xh = lax.axis_index("xh")
    half = 1 - xh if part == 0 else xh
    row = ((half * 8 + z) * 2 + lax.axis_index("core")) * ROWS
    return row + lax.broadcasted_iota(jnp.int32, (ROWS, lanes), 0)


def unpack_rows(x, z, dst):
    left, right = x[:, 0:HSIZE], x[:, HSIZE:128]
    at, end = z * 128, 1024 + z * 64
    dst[at : at + 96, :] = left
    dst[at + 96 : at + 128, :] = right[0:32]
    dst[end : end + 64, :] = right[32:96]


def turn_rows(dqt, dq, put):
    for b in range(3):
        dq[b * 512 : b * 512 + 512, :] = dqt[:, b * 512 : b * 512 + 512].T
    for z in range(8):
        at, end = z * 128, 1024 + z * 64
        put(z, slice(0, 96), slice(0, HSIZE), dq[at : at + 96, :])
        put(z, slice(0, 32), slice(HSIZE, 128), dq[at + 96 : at + 128, :])
        put(z, slice(32, 96), slice(HSIZE, 128), dq[end : end + 64, :])


def prep_queries(x_ref, q_ref, do_ref, st_ref):
    lane = lax.broadcasted_iota(jnp.int32, (1, 128), 1)
    stats = []
    for z in range(8):
        unpack_rows(x_ref[z, 0:HALF, :], z, q_ref)
        unpack_rows(x_ref[z, HALF:ROWS, :], z, do_ref)
        st = x_ref[z, ROWS : ROWS + 16, :].astype(F32)
        st_ref[0:1, z * 128 : z * 128 + 128] = st[0:1]
        st_ref[1:2, z * 128 : z * 128 + 128] = st[2:3]
        stats.append(st)
    for m in range(4):
        a, b = stats[2 * m], stats[2 * m + 1]
        at = 1024 + m * 128
        for row in range(2):
            src = 2 * row + 1
            st_ref[row : row + 1, at : at + 128] = jnp.where(
                lane < 64, a[src : src + 1], pltpu.roll(b[src : src + 1], 64, 1)
            )


def prep_keys(part, lengths_ref, x_ref, k_ref, v_ref, kt_ref, kf):
    length = record_length(lengths_ref)
    for z in range(8):
        kv = x_ref[z]
        rows = slice(z * ROWS, z * ROWS + ROWS)
        k_ref[rows, :] = kv[:, 0:HSIZE]
        v_ref[rows, :] = kv[:, HSIZE:128]
        kf[rows, :] = jnp.where(key_rows(part, z, 128) < length, kv.astype(F32) * 0.125, 0.0)
    for b in range(3):
        turned = kf[b * 512 : b * 512 + 512, :].T
        kt_ref[:, b * 512 : b * 512 + 512] = turned[0:HSIZE].astype(BF)


def score_tile(q, do, st, k, v, kt, dqt, dks, dvs):
    def key_block(ui, _):
        u0 = pl.multiple_of(ui * BU, BU)
        kb = k[pl.ds(u0, BU), :]
        vb = v[pl.ds(u0, BU), :]
        ktb = kt[:, pl.ds(u0, BU)]
        qb, dob = q[...], do[...]
        s = lax.dot_general(kb, qb, NT, preferred_element_type=F32)
        p = jnp.exp(s - st[1:2, :])
        dp = lax.dot_general(vb, dob, NT, preferred_element_type=F32)
        ds = (p * (dp - st[0:1, :])).astype(BF)
        dvs[pl.ds(u0, BU), :] += lax.dot_general(p.astype(BF), dob, NN, preferred_element_type=F32)
        dks[pl.ds(u0, BU), :] += lax.dot_general(ds, qb, NN, preferred_element_type=F32)
        dqt[...] += lax.dot_general(ktb, ds, NN, preferred_element_type=F32)
        return 0

    lax.fori_loop(0, CHUNK // BU, key_block, 0)


def tile_1(q, do, st, k, v, kt, dqt, dks, dvs):
    for ref in (dqt, dks, dvs):
        ref[...] = jnp.zeros_like(ref)
    score_tile(q, do, st, k, v, kt, dqt, dks, dvs)


def pack_queries(dqt, dq, dq_ref):
    def put(z, rows, cols, value):
        dq_ref[z, rows, cols] = value.astype(BF)

    turn_rows(dqt, dq, put)


def pack_keys(part, lengths_ref, dks, dvs, dkv_ref):
    length = record_length(lengths_ref)
    for z in range(8):
        keep = key_rows(part, z, HSIZE) < length
        rows = slice(z * ROWS, z * ROWS + ROWS)
        dkv_ref[z, :, 0:HSIZE] = jnp.where(keep, dks[rows, :], 0.0).astype(BF)
        dkv_ref[z, :, HSIZE:128] = jnp.where(keep, dvs[rows, :], 0.0).astype(BF)


def tile_2(q, do, st, k, v, kt, dq_in, dq_ref, dks, dvs, dqt, dq):
    dqt[...] = dq_in[...]
    dks[...] = jnp.zeros_like(dks)
    dvs[...] = jnp.zeros_like(dvs)
    score_tile(q, do, st, k, v, kt, dqt, dks, dvs)
    pack_queries(dqt, dq, dq_ref)


def tile_3(lengths_ref, q, do, st, k, v, kt, dk_ref, dv_ref, dkv_ref, dqt, dks, dvs):
    dqt[...] = jnp.zeros_like(dqt)
    dks[...] = dk_ref[...]
    dvs[...] = dv_ref[...]
    score_tile(q, do, st, k, v, kt, dqt, dks, dvs)
    pack_keys(0, lengths_ref, dks, dvs, dkv_ref)


def tile_4(
    lengths_ref, q, do, st, k, v, kt, dq_in, dk_ref, dv_ref, dq_ref, dkv_ref, dks, dvs, dqt, dq
):
    dqt[...] = dq_in[...]
    dks[...] = dk_ref[...]
    dvs[...] = dv_ref[...]
    score_tile(q, do, st, k, v, kt, dqt, dks, dvs)
    pack_queries(dqt, dq, dq_ref)
    pack_keys(1, lengths_ref, dks, dvs, dkv_ref)


def tile_call(body, lengths, args, outs, scratch=()):
    whole = lambda x: pl.BlockSpec(x.shape, lambda *_: (0,) * len(x.shape))
    specs = [whole(a) for a in args]
    if lengths is not None:
        specs.insert(0, pl.BlockSpec(memory_space=pltpu.SMEM))
        args = (lengths,) + args
    return call(
        body,
        outs,
        7,
        40,
        grid=(1,),
        in_specs=specs,
        out_specs=tuple(whole(o) for o in outs),
        scratch_shapes=scratch,
    )(*args)


def combine(dkv_ref, dkv_got_ref, dq_ref, dq_got_ref, o_ref):
    o_ref[:, 0:ROWS, :] = (dkv_ref[...].astype(F32) + dkv_got_ref[...].astype(F32)).astype(BF)
    o_ref[:, ROWS:, :] = (dq_ref[...].astype(F32) + dq_got_ref[...].astype(F32)).astype(BF)


def unpack_final(x_ref, q_ref, k_ref, v_ref):
    for h in range(HEADS):
        cols = slice(h * HSIZE, (h + 1) * HSIZE)
        k_ref[0, :, cols] = x_ref[h, 0:ROWS, 0:HSIZE]
        v_ref[0, :, cols] = x_ref[h, 0:ROWS, HSIZE:128]
        q_ref[0, 0:HALF, cols] = x_ref[h, ROWS : ROWS + HALF, 0:HSIZE]
        q_ref[0, HALF:ROWS, cols] = x_ref[h, ROWS : ROWS + HALF, HSIZE:128]


def finish_sums(lengths_ref, own_ref, got_ref, proj_ref, taps_ref):
    total = lengths_ref[0]
    for r in range(1, 8):
        total = total + lengths_ref[r]
    scale = lax.rsqrt(jnp.full((1, 128), total, jnp.int32).astype(F32))
    core = lax.axis_index("core")
    for c in range(8):
        cols = slice(c * 128, c * 128 + 128)
        own, got = own_ref[c % 4].astype(F32), got_ref[c % 4].astype(F32)
        x = jnp.where(core == c // 4, own, got) * scale
        proj_ref[:, cols] = x[0:512]
        taps_ref[:, cols] = x[512:543]


def flip(x, axis, mask, size):
    return lax.ppermute(x, axis, [(i, i ^ mask) for i in range(size)])


def add(*terms):
    pair = [a.astype(F32) + b.astype(F32) for a, b in zip(terms[::2], terms[1::2])]
    return (pair[0] if len(pair) == 1 else pair[0] + pair[1]).astype(BF)


def reduce_dp(x, shift, count):
    me = (lax.axis_index("dp") >> shift) & (count - 1)
    pieces = x.reshape(count, x.shape[0] // count, 128)
    piece = lambda i: lax.dynamic_index_in_dim(pieces, i, 0, keepdims=False)
    got = [flip(piece(me ^ d), "dp", d << shift, 8) for d in range(1, count)]
    return add(piece(me), *got)


def sum_four(x, low, high, beside):
    got = [flip(x, ("xh", "z"), mask, 16) for mask in (low, high, low | high)]
    return add(after(x, beside), *got)


def sum_two(x, mask, beside):
    return add(after(x, beside), flip(x, ("xh", "z"), mask, 16))


def gather_y(x, beside):
    y = lax.axis_index("dp") >> 1
    odd, upper = (y & 1) == 1, (y & 2) == 2
    b, c, d = [flip(x, "dp", m << 1, 8) for m in (1, 2, 3)]
    a = after(x, beside)
    low = jnp.concatenate([jnp.where(odd, b, a), jnp.where(odd, a, b)], axis=0)
    high = jnp.concatenate([jnp.where(odd, d, c), jnp.where(odd, c, d)], axis=0)
    return jnp.concatenate([jnp.where(upper, high, low), jnp.where(upper, low, high)], axis=0)


def gather_x(x, beside):
    odd = (lax.axis_index("dp") & 1) == 1
    got = flip(x, "dp", 1, 8)
    x = after(x, beside)
    return jnp.concatenate([jnp.where(odd, got, x), jnp.where(odd, x, got)], axis=0)


def after(x, *first):
    return lax.optimization_barrier((x,) + first)[0]


def swap(x, axis):
    return lax.ppermute(x, axis, [(0, 1), (1, 0)])


def shards(query, key, value, attn, log, lengths, x, g, proj, taps):
    smem = pl.BlockSpec(memory_space=pltpu.SMEM)
    vmem = pl.BlockSpec(memory_space=pltpu.VMEM)
    up = [(i, i + 1) for i in range(31)]
    down = [(i + 1, i) for i in range(31)]
    last, first = rims_call(x, g)
    lo = lax.ppermute(last, SEQ, up)
    hi = lax.ppermute(first, SEQ, down)
    grad_state, sums, pay = conv_call(
        lengths, x, g, lo, hi, taps, proj, attn, log[0].T, query, key, value
    )
    pay = lax.all_to_all(pay, "z", 0, 0, tiled=True)

    core = lax.axis_index("core")
    sums = sums.reshape(2, 2176, 128)
    send = lax.dynamic_index_in_dim(sums, 1 - core, 0, keepdims=False)
    keep = lax.dynamic_index_in_dim(sums, core, 0, keepdims=False)
    sums = add(keep, swap(send, "core"))
    sums = reduce_dp(sums, 0, 2)
    sums = reduce_dp(sums, 1, 4)

    queries, keys = pay[:, ROWS:], pay[:, :ROWS]
    core_queries, other_keys = swap(queries, "core"), swap(keys, "xh")

    half = sds((CHUNK, HSIZE))

    def prepared_queries(x):
        return call(prep_queries, (half, half, sds((8, CHUNK), F32)), 1, 8)(x)

    def prepared_keys(part, x):
        return call(
            functools.partial(prep_keys, part),
            (half, half, sds((HSIZE, CHUNK))),
            1,
            8,
            in_specs=[smem, vmem],
            scratch_shapes=[pltpu.VMEM((CHUNK, 128), F32)],
        )(lengths, x)

    qo = prepared_queries(queries)
    ko = prepared_keys(1, keys)
    grad = sds((CHUNK, HSIZE), F32)
    turned = sds((HSIZE, CHUNK), F32)
    fgrad = pltpu.VMEM((CHUNK, HSIZE), F32)
    fturned = pltpu.VMEM((HSIZE, CHUNK), F32)
    dqo, dk, dv = tile_call(tile_1, None, qo + ko, (turned, grad, grad))
    sums = sum_four(sums, 1, 8, dk)

    kx = prepared_keys(0, other_keys)
    dqo = after(dqo, sums)
    packed_q = sds((8, HALF, 128))
    packed_k = sds((HEADS, ROWS, 128))
    dqo, dkx, dvx = tile_call(
        tile_2, None, qo + kx + (dqo,), (packed_q, grad, grad), [fturned, fgrad]
    )
    sums = sum_two(sums, 2, dvx)

    qc = prepared_queries(core_queries)
    dkx = after(dkx, sums)
    dkv_other, dqc = tile_call(
        tile_3, lengths, qc + kx + (dkx, dvx), (packed_k, turned), [fgrad, fgrad]
    )
    dkv_got = swap(dkv_other, "xh")
    sums = sum_two(sums, 4, dqc)
    dqc = after(dqc, sums)
    dq_core, dkv_own = tile_call(
        tile_4,
        lengths,
        qc + ko + (dqc, dk, dv),
        (packed_q, packed_k),
        [fgrad, fgrad, fturned, fgrad],
    )
    dq_got = swap(dq_core, "core")
    back = call(
        combine, sds((HEADS, ROWS + HALF, 128)), 1, 8, in_specs=[vmem] * 4
    )(dkv_own, dkv_got, dqo, dq_got)

    sums = gather_x(gather_y(sums, dkv_own), back)
    back = lax.all_to_all(back, "z", 0, 0, tiled=True)
    sums = sums.reshape(4, 544, 128)
    grad_proj, grad_taps = call(
        finish_sums,
        (sds((512, 1024), F32), sds((TAPS, 1024), F32)),
        2,
        8,
        in_specs=[smem, vmem, vmem],
    )(lengths, sums, swap(sums, "core"))
    grad_q, grad_k, grad_v = call(unpack_final, (sds((1, ROWS, 512)),) * 3, 2, 8)(back)
    return grad_q, grad_k, grad_v, grad_state, grad_proj, grad_taps


def solution(mesh):
    inner = Mesh(mesh.devices.reshape(8, 2, 8, 2), ALL)
    rows = P("dp", SEQ, None)
    in_specs = (rows,) * 5 + (P(), rows, rows, P(), P())
    out_specs = (rows,) * 4 + (P(), P())
    return jax.shard_map(
        shards, mesh=inner, in_specs=in_specs, out_specs=out_specs, check_vma=False
    )
```
